256 devices in a mesh: lon: 32 (over y_lo, z, core), lat: 8 (over x, y_hi).
Axes of the slice: x: 4, y: 4 (y_hi: 2, y_lo: 2; y = y_hi * 2 + y_lo), z: 8, core: 2. Of those that a mesh axis runs over, the one named last changes fastest.
Arguments:
- perturbations: float32 [2, 16, 1024, 4096], P(None, None, 'lat', 'lon'), may hold values from -6 to 6
- zonal_rate: float32 [2, 2, 4096], P(None, None, 'lon'), may hold values from 0.5 to 1, as said below
- meridional_rate: float32 [2, 2, 1024], replicated, may hold values from 0.5 to 1, as said below
- amplitude: float32 [2, 2, 1024, 4096], P(None, None, 'lat', 'lon'), may hold values from 1 to 10
Outputs:
- localized: float32 [2, 16, 1024, 4096], P(None, None, 'lat', 'lon')
The draws below stay inside these ranges and needn't reach their ends.
Inputs may be any that keep to these rules, and one draw needn't show every extreme that they name: `zonal_rate`: every entry is greater than 0.5 and at most 1 - 0.15 / 4096. `meridional_rate`: every entry is greater than 0.5 and at most 1 - 0.15 / 1024.
All inputs are finite; a program needn't handle non-finite values.
Results may differ from the reference program's by a relative error of at most 0.0003.
Values sent between devices are 32-bit elements; how exact they have to be, the bound alone decides.
A program may use at most 64 MiB of HBM per device.

```python
import math
import jax
import jax.numpy as jnp
from jax import lax

MEM = 16
LEV = 2
SCALES = 2
NLON = 4096
NLAT = 1024


def rate_draw(key, length):
    seed_handles = jax.random.split(key, 7)
    tensor_extents = (SCALES, LEV)
    slow = jax.random.uniform(seed_handles[0], tensor_extents) > 0.5
    spread = jnp.exp(jax.random.uniform(seed_handles[1], tensor_extents, jnp.float32, jnp.log(0.3), jnp.log(1.2)))
    slow_loss = spread / length
    fast_loss = 1.0 / jax.random.uniform(seed_handles[2], tensor_extents, jnp.float32, 30.0, 50.0)
    loss = jnp.where(slow, slow_loss, fast_loss)[..., None]
    rough = jnp.exp(jax.random.uniform(seed_handles[3], tensor_extents + (length,), jnp.float32, jnp.log(0.5), jnp.log(2.0)))
    rate = 1.0 - loss * rough
    front_slot = jax.random.randint(seed_handles[4], tensor_extents, 0, length)
    offset = jax.random.randint(seed_handles[6], tensor_extents, 1, length)
    rear_slot = (front_slot + offset) % length
    spike_site_index = jnp.stack([front_slot, rear_slot], axis=-1)
    spike_gain = jax.random.uniform(seed_handles[5], tensor_extents + (2,), jnp.float32, 0.6, 0.85)
    grid_slots = jnp.arange(length)
    agreeing_tally = grid_slots[None, None, None, :] == spike_site_index[..., None]
    length_ratios = jnp.prod(jnp.where(agreeing_tally, spike_gain[..., None], 1.0), axis=2)
    return (rate * length_ratios).astype(jnp.float32)


def draw_zonal_rate(key, part):
    return rate_draw(jax.random.fold_in(key, 11), NLON)


def draw_meridional_rate(key, part):
    return rate_draw(jax.random.fold_in(key, 12), NLAT)


def steps_of(own_key, dims, cuts, smallest, largest):
    level = 1.0
    for position, blocks in cuts:
        draws = jax.random.uniform(jax.random.fold_in(jax.random.fold_in(own_key, 6), position), (blocks,), jnp.float32, smallest / len(cuts), largest / len(cuts))
        level = level * jnp.repeat(jnp.exp(draws), dims[position] // blocks).reshape((-1,) + (1,) * (len(dims) - 1 - position))
    return level


def bell_draw(rng, dims, deviation, most, shards=(), dtype=jnp.bfloat16):
    drawn = jax.random.normal(rng, dims, jnp.float32) * deviation
    if len(shards) > 0:
        drawn = steps_of(rng, dims, shards, -0.22, 0.18) * drawn
    return jnp.clip(drawn, min=-most, max=most).astype(dtype)


def setup_inputs(seed: int = 0) -> dict:
    seeds = jax.random.split(jax.random.key(seed), 5)
    perturbations = bell_draw(seeds[0], (LEV, MEM, NLAT, NLON), 1.0, 6.0, ((2, 8), (3, 32)), jnp.float32)
    zonal_rate = draw_zonal_rate(jax.random.fold_in(seeds[4], 71), 0)
    meridional_rate = draw_meridional_rate(jax.random.fold_in(seeds[4], 71), 0)
    amplitude = jnp.clip(jnp.exp(math.log(10.0) - 2.3025851 * jax.random.uniform(seeds[3], (SCALES, LEV, NLAT, NLON), jnp.float32) ** steps_of(seeds[3], (SCALES, LEV, NLAT, NLON), ((2, 8), (3, 32)), -0.2, 0.2)), 1.0, 10.0)
    return dict(perturbations=perturbations, zonal_rate=zonal_rate, meridional_rate=meridional_rate, amplitude=amplitude)


def open_pass(field, rate, reverse):
    def advance(carry, inputs):
        value, factor = inputs
        carry = factor * carry + (1.0 - factor) * value
        return carry, carry

    start = jnp.zeros(field.shape[1:], jnp.float32)
    _, result = lax.scan(advance, start, (field, rate), reverse=reverse)
    return result


def periodic_pass(field, rate, reverse):
    result = open_pass(field, rate, reverse)
    if reverse:
        growth = jnp.cumprod(rate[::-1], axis=0)[::-1]
        whole = growth[0]
        closing = result[0] / (1.0 - whole)
    else:
        growth = jnp.cumprod(rate, axis=0)
        whole = growth[-1]
        closing = result[-1] / (1.0 - whole)
    return result + growth * closing[None]


def reference(perturbations, zonal_rate, meridional_rate, amplitude):
    total = jnp.zeros(perturbations.shape, jnp.float32)
    for scale in range(SCALES):
        field = jnp.transpose(perturbations, (3, 0, 1, 2))
        rate = jnp.transpose(zonal_rate[scale])[:, :, None, None]
        for sweep in range(2):
            field = periodic_pass(field, rate, False)
            field = periodic_pass(field, rate, True)
        field = jnp.transpose(field, (3, 1, 2, 0))
        rate = jnp.transpose(meridional_rate[scale])[:, :, None, None]
        for sweep in range(2):
            field = open_pass(field, rate, False)
            field = open_pass(field, rate, True)
        field = jnp.transpose(field, (1, 2, 0, 3))
        total = total + amplitude[scale][:, None] * field
    return total
```

```python
import functools

import jax
import jax.numpy as jnp
from jax import lax
from jax.experimental import pallas as pl
from jax.experimental.pallas import tpu as pltpu
from jax.sharding import PartitionSpec as P

MESH = pl.DeviceIdType.MESH
F32, BF16 = jnp.float32, jnp.bfloat16
HIGHEST = lax.Precision.HIGHEST

NN = (((1,), (0,)), ((), ()))
NT = (((1,), (1,)), ((), ()))
TN = (((0,), (0,)), ((), ()))


def halves(x):
    high = x.astype(BF16)
    return high, (x - high.astype(F32)).astype(BF16)


def mul(a, b, dims):
    return lax.dot_general(a, b, dims, preferred_element_type=F32)


def dot3(a, b, dims):
    ah, al = halves(a)
    bh, bl = halves(b)
    ka, kb = dims[0][0][0], dims[0][1][0]
    return mul(jnp.concatenate([ah, al], ka), jnp.concatenate([bh, bh], kb), dims) + mul(
        ah, bl, dims
    )


def lane(shape):
    return lax.broadcasted_iota(jnp.int32, shape, 1)


def row(shape):
    return lax.broadcasted_iota(jnp.int32, shape, 0)


def scan_lanes(v, steps, sign):
    width = v.shape[1]
    for k, factor in steps:
        v = v + factor * pltpu.roll(v, k if sign > 0 else width - k, 1)
    return v


def solve(states, coupling, blocks, cyclic):
    g, r, e1e2, w1e2, e1w2, w1w2 = coupling
    shape = (blocks, 128)
    at = row(shape)
    levels = blocks.bit_length() - 1

    def shifted(x, k):
        moved = pltpu.roll(x, k % blocks, 0)
        if cyclic:
            return moved
        return jnp.where((at >= k) if k > 0 else (at < blocks + k), moved, 0.0)

    factors = {}
    for sign in (1, -1):
        a = pltpu.roll(g, sign % blocks, 0)
        factors[sign] = []
        for level in range(levels):
            factors[sign].append(a)
            a = a * pltpu.roll(a, (sign * 2**level) % blocks, 0)
        factors[sign].append(1.0 / (1.0 - a) if cyclic else None)

    def carry(parts, sign):
        out = []
        for v in parts:
            v = shifted(v, sign)
            for level in range(levels):
                v = v + factors[sign][level] * shifted(v, sign * 2**level)
            out.append(v * factors[sign][levels] if cyclic else v)
        return out

    n = len(states[0])
    e1 = carry(states[0], 1)
    w1 = carry([states[1][i] + r * e1[i] for i in range(n)], -1)
    e2 = carry([states[2][i] + e1e2 * e1[i] + w1e2 * w1[i] for i in range(n)], 1)
    w2 = carry(
        [states[3][i] + e1w2 * e1[i] + w1w2 * w1[i] + r * e2[i] for i in range(n)], -1
    )
    return e1, w1, e2, w2


def kernel(
    nz, nm, mem, split1, split2,
    x_hbm, zr_ref, mr_ref, amp_hbm, out_ref,
    x_ref, amp_ref, field,
    vz_ref, vm_ref, uz_ref, um_ref,
    az_wide, az_low, am_wide, am_low,
    qs, qr, rs, rin, ps, pr, prs, pin,
    kz_own, kz_all, km_own, km_all, crs, crr, centre,
    lq_ref, d_ref, cr_tile,
    load_sem, send_sem, recv_sem,
):
    zi, mi = lax.axis_index("lon"), lax.axis_index("lat")
    rows = 16 * mem
    zrows, mrows = rows // nz, rows // nm
    per_pair = 4 * mem

    barrier = pltpu.get_barrier_semaphore()

    def greet_lon(k, _):
        pl.semaphore_signal(
            barrier, inc=1, device_id={"lon": lax.rem(zi + k, nz)}, device_id_type=MESH
        )
        return 0

    def greet_lat(k, _):
        pl.semaphore_signal(
            barrier, inc=1, device_id={"lat": lax.rem(mi + k, nm)}, device_id_type=MESH
        )
        return 0

    lax.fori_loop(1, nz, greet_lon, 0)
    lax.fori_loop(1, nm, greet_lat, 0)
    x_copy = pltpu.make_async_copy(x_hbm, x_ref, load_sem.at[0])
    amp_copy = pltpu.make_async_copy(amp_hbm, amp_ref, load_sem.at[1])
    x_copy.start()
    amp_copy.start()

    own = pl.ds(pl.multiple_of(mi * 128, 128), 128)
    a = jnp.concatenate(
        [zr_ref[0], zr_ref[1], mr_ref[0, :, own], mr_ref[1, :, own]], axis=0
    )
    loss = 1.0 - a
    la = jnp.log(a)
    square = (128, 128)
    upto = jnp.where(row(square) <= lane(square), 1.0, 0.0)
    li = lax.dot_general(la, upto, NN, precision=HIGHEST, preferred_element_type=F32)
    lx = li - la
    total = li[:, 127:128]
    at = lane((8, 128))
    east_cols, west_cols, east_rows, west_rows = [], [], [], []
    for p in range(7):
        k = 2**p
        back = pltpu.roll(li, k, 1)
        ahead = pltpu.roll(li, 128 - k, 1)
        xback = pltpu.roll(lx, k, 1)
        xahead = pltpu.roll(lx, 128 - k, 1)
        first, last = at >= k, at < 128 - k
        east_cols.append((k, jnp.where(first, jnp.exp(jnp.where(first, li - back, 0.0)), 0.0)))
        east_rows.append((k, jnp.where(last, jnp.exp(jnp.where(last, ahead - li, 0.0)), 0.0)))
        west_cols.append((k, jnp.where(last, jnp.exp(jnp.where(last, xahead - lx, 0.0)), 0.0)))
        west_rows.append((k, jnp.where(first, jnp.exp(jnp.where(first, lx - xback, 0.0)), 0.0)))

    def rows_east(v):
        return loss * scan_lanes(v, east_rows, -1)

    def rows_west(v):
        return loss * scan_lanes(v, west_rows, 1)

    def cols_east(x):
        return scan_lanes(loss * x, east_cols, 1)

    def cols_west(x):
        return scan_lanes(loss * x, west_cols, -1)

    ge = jnp.exp(li)
    gw = jnp.exp(total - lx)
    v1 = jnp.exp(total - li) * loss
    w0 = jnp.exp(lx) * loss
    v2 = rows_east(w0)
    x1 = rows_west(v1)
    v3 = rows_east(x1)
    x2 = rows_west(v2)
    v4 = rows_east(x2)

    def along(v):
        return jnp.sum(v, axis=1, keepdims=True)

    kinds = (
        jnp.exp(total), along(w0 * ge), along(x1 * ge),
        along(v1 * gw), along(x2 * ge), along(v2 * gw),
    )
    packed = jnp.zeros((8, 128), F32)
    for k, value in enumerate(kinds):
        packed = jnp.where(at == k, value, packed)
    for n in range(4):
        kz_own[n] = packed[n : n + 1]
    km_own[0:4] = packed[4:8]
    km_own[4:8] = packed[4:8]
    for f, v in enumerate((v1, v2, v3, v4)):
        for n in range(4):
            vz_ref[n * 4 + f : n * 4 + f + 1, :] = v[n : n + 1]
            vm_ref[n * 4 + f : n * 4 + f + 1, :] = v[4 + n : 5 + n]

    x_copy.wait()
    for l in range(2):
        both = [
            jnp.concatenate([ref[l * 4 : l * 4 + 4], ref[8 + l * 4 : 12 + l * 4]], axis=0)
            for ref in (vz_ref, vm_ref)
        ]
        zh, zl = halves(both[0])
        mh, ml = halves(both[1])
        z_wide = jnp.concatenate([zh, zl], axis=1)
        m_wide = jnp.concatenate([mh, ml], axis=1)

        def states(m, _):
            xh, xl = halves(x_ref[l, m])
            q = mul(z_wide, jnp.concatenate([xh, xh], axis=1), NT) + mul(zh, xl, NT)
            p = mul(m_wide, jnp.concatenate([xh, xh], axis=0), NN) + mul(mh, xl, NN)
            for s in range(2):
                base = (s * 2 + l) * per_pair
                qs[pl.ds(base + m * 4, 4), :] = q[s * 4 : s * 4 + 4]
                ps[pl.ds(base + m * 4, 4), :] = p[s * 4 : s * 4 + 4]
            return 0

        lax.fori_loop(0, mem, states, 0, unroll=4)

    pl.semaphore_wait(barrier, nz + nm - 2)

    def chunk(ref, index, size):
        return ref.at[pl.ds(pl.multiple_of(index * size, size), size), :]

    def remote(src, dst, which, **device):
        return pltpu.make_async_remote_copy(
            src_ref=src, dst_ref=dst,
            send_sem=send_sem.at[which], recv_sem=recv_sem.at[which],
            device_id=device, device_id_type=MESH,
        )

    other_z, other_m = lax.rem(zi + 1, nz), lax.rem(mi + 1, nm)

    def send_lon(k, _):
        d = lax.rem(zi + k, nz)
        remote(kz_own.at[d * zrows // per_pair], kz_all.at[zi], 1, lon=d).start()
        remote(chunk(qs, d, zrows), chunk(qr, zi, zrows), 0, lon=d).start()
        return 0

    def send_lat(k, _):
        d = lax.rem(mi + k, nm)
        remote(chunk(ps, d, mrows), chunk(pr, mi, mrows), 2, lat=d).start()
        remote(km_own, chunk(km_all, mi, 8), 3, lat=d).start()
        return 0

    lax.fori_loop(1, nz, send_lon, 0)
    lax.fori_loop(1, nm, send_lat, 0)
    kz_all[zi] = kz_own[zi * zrows // per_pair]
    chunk(qr, zi, zrows)[...] = chunk(qs, zi, zrows)[...]
    chunk(pr, mi, mrows)[...] = chunk(ps, mi, mrows)[...]
    chunk(km_all, mi, 8)[...] = km_own[...]

    u3 = cols_west(ge)
    u2 = cols_west(cols_east(gw))
    u1 = cols_west(cols_east(u3))
    for f, u in enumerate((u1, u2, u3, gw)):
        for n in range(4):
            uz_ref[n * 4 + f : n * 4 + f + 1, :] = u[n : n + 1]
            um_ref[n * 4 + f : n * 4 + f + 1, :] = u[4 + n : 5 + n]

    lit, lxt = jnp.transpose(li), jnp.transpose(lx)
    below = row(square) >= lane(square)
    above = row(square) <= lane(square)
    for n in range(8):
        down = jnp.where(below, lit[:, n : n + 1] - li[n : n + 1], 0.0)
        up = jnp.where(above, lx[n : n + 1] - lxt[:, n : n + 1], 0.0)
        east = jnp.where(below, jnp.exp(down), 0.0) * loss[n : n + 1]
        west = jnp.where(above, jnp.exp(up), 0.0) * loss[n : n + 1]
        once = dot3(west, east, NN)
        high, low = halves(dot3(once, once, NN))
        if n < 4:
            s, l = n // 2, n % 2
            az_wide[l, s * 128 : s * 128 + 128, 0:128] = high
            az_wide[l, s * 128 : s * 128 + 128, 128:256] = high
            az_low[l, s * 128 : s * 128 + 128, :] = low
        else:
            am_wide[n - 4, :, 0:128] = high
            am_wide[n - 4, :, 128:256] = high
            am_low[n - 4] = low

    def local_pass(i, _):
        l, m = i // mem, lax.rem(i, mem)
        xh, xl = halves(x_ref[l, m])
        f = mul(jnp.concatenate([xh, xl], axis=1), az_wide[l], NT) + mul(xh, az_low[l], NT)
        for s in range(2):
            n = s * 2 + l
            fh, fl = halves(f[:, s * 128 : s * 128 + 128])
            field[n, m] = mul(am_wide[n], jnp.concatenate([fh, fl], axis=0), NN) + mul(
                am_low[n], fh, NN
            )
        return 0

    lax.fori_loop(0, split1, local_pass, 0, unroll=2)

    zshape, mshape = (nz, 128), (nm, 128)
    remote(qs.at[pl.ds(0, (nz - 1) * zrows)], qr.at[pl.ds(0, (nz - 1) * zrows)], 0, lon=other_z).wait()
    remote(kz_all.at[pl.ds(0, nz - 1)], kz_all.at[pl.ds(0, nz - 1)], 1, lon=other_z).wait()
    kz = kz_all[...].reshape(nz, 128)
    coupling = [jnp.broadcast_to(kz[:, k : k + 1], zshape) for k in range(6)]
    groups = zrows // 4
    got = [
        [qr[pl.ds(g * 4 + f, nz, stride=zrows), :] for g in range(groups)] for f in range(4)
    ]
    for f, parts in enumerate(solve(got, coupling, nz, True)):
        for g in range(groups):
            rs[pl.ds(g * 4 + f, nz, stride=zrows), :] = parts[g]

    def back_lon(k, _):
        d = lax.rem(zi + k, nz)
        remote(chunk(rs, d, zrows), chunk(rin, zi, zrows), 4, lon=d).start()
        return 0

    lax.fori_loop(1, nz, back_lon, 0)
    chunk(rin, zi, zrows)[...] = chunk(rs, zi, zrows)[...]

    remote(ps.at[pl.ds(0, (nm - 1) * mrows)], pr.at[pl.ds(0, (nm - 1) * mrows)], 2, lat=other_m).wait()
    remote(km_all.at[pl.ds(0, (nm - 1) * 8)], km_all.at[pl.ds(0, (nm - 1) * 8)], 3, lat=other_m).wait()
    pair = mi * mrows // per_pair
    km = [km_all[pl.ds(n, nm, stride=8), :] for n in range(4)]
    mine = km[0]
    for n in range(1, 4):
        mine = jnp.where(pair == n, km[n], mine)
    coupling = [jnp.broadcast_to(mine[:, k : k + 1], mshape) for k in range(6)]
    groups = mrows // 4
    got = [
        [pr[pl.ds(g * 4 + f, nm, stride=mrows), :] for g in range(groups)] for f in range(4)
    ]
    for f, parts in enumerate(solve(got, coupling, nm, False)):
        for g in range(groups):
            prs[pl.ds(g * 4 + f, nm, stride=mrows), :] = parts[g]

    def back_lat(k, _):
        d = lax.rem(mi + k, nm)
        remote(chunk(prs, d, mrows), chunk(pin, mi, mrows), 5, lat=d).start()
        return 0

    lax.fori_loop(1, nm, back_lat, 0)
    chunk(pin, mi, mrows)[...] = chunk(prs, mi, mrows)[...]

    lax.fori_loop(split1, split2, local_pass, 0, unroll=2)

    remote(rs.at[pl.ds(0, (nz - 1) * zrows)], rin.at[pl.ds(0, (nz - 1) * zrows)], 4, lon=other_z).wait()
    cross = dot3(vm_ref[...], rin[...], NT)
    wide = (16, rows)
    cross = jnp.where(row(wide) // 4 == lane(wide) // per_pair, cross, 0.0)
    cross = cross[0:4] + cross[4:8] + cross[8:12] + cross[12:16]
    crs[0:4] = cross[:, 0:128]
    crs[4:8] = cross[:, 128:256]

    def send_cross(k, _):
        d = lax.rem(mi + k, nm)
        remote(crs, chunk(crr, mi, 8), 6, lat=d).start()
        return 0

    lax.fori_loop(1, nm, send_cross, 0)
    chunk(crr, mi, 8)[...] = crs[...]

    lax.fori_loop(split2, 2 * mem, local_pass, 0, unroll=2)

    remote(prs.at[pl.ds(0, (nm - 1) * mrows)], pin.at[pl.ds(0, (nm - 1) * mrows)], 5, lat=other_m).wait()
    for n in range(4):
        s, l = n // 2, n % 2
        part = slice(n * per_pair, (n + 1) * per_pair)
        ph, plow = halves(pin[part])
        d_ref[part] = mul(
            jnp.concatenate([ph, plow], axis=1), az_wide[l, s * 128 : s * 128 + 128, :], NT
        ) + mul(ph, az_low[l, s * 128 : s * 128 + 128, :], NT)
        qh, ql = halves(rin[part])
        lq_ref[part] = mul(jnp.concatenate([qh, ql], axis=1), am_wide[n], NT) + mul(
            qh, am_low[n], NT
        )
    amp_copy.wait()

    remote(crr.at[pl.ds(0, (nm - 1) * 8)], crr.at[pl.ds(0, (nm - 1) * 8)], 6, lat=other_m).wait()
    for h in range(2):
        left = lane(mshape) < per_pair
        coupling = [
            jnp.where(left, km[2 * h][:, k : k + 1], km[2 * h + 1][:, k : k + 1])
            for k in range(6)
        ]
        got = [[crr[pl.ds(h * 4 + f, nm, stride=8), :]] for f in range(4)]
        for f, parts in enumerate(solve(got, coupling, nm, False)):
            centre[h * 4 + f] = parts[0]
    for n in range(4):
        h = n // 2
        for f in range(4):
            line = centre[h * 4 + f, pl.ds(mi, 1), :]
            line = jnp.where(lane((1, 128)) // per_pair == n % 2, line, 0.0)
            r = n * 4 + f
            cr_tile[r : r + 1, h * 128 : h * 128 + 128] = line
            cr_tile[r : r + 1, (1 - h) * 128 : (1 - h) * 128 + 128] = jnp.zeros((1, 128), F32)
    lq_ref[...] += dot3(cr_tile[...], um_ref[...], TN)

    def finish(i, _):
        l, m = i // mem, lax.rem(i, mem)
        result = None
        for s in range(2):
            n = s * 2 + l
            part = pl.ds(n * per_pair + m * 4, 4)
            resp = pl.ds(n * 4, 4)
            left = jnp.concatenate([lq_ref[part, :], um_ref[resp, :]], axis=0)
            right = jnp.concatenate([uz_ref[resp, :], d_ref[part, :]], axis=0)
            lh = left.astype(BF16).astype(F32)
            rh = right.astype(BF16).astype(F32)
            stacked_left = jnp.concatenate([lh, left - lh, lh], axis=0).astype(BF16)
            stacked_right = jnp.concatenate([rh, rh, right - rh], axis=0).astype(BF16)
            y = field[n, m] + mul(stacked_left, stacked_right, TN)
            y = y * amp_ref[s, l]
            result = y if result is None else result + y
        out_ref[l, m] = result
        return 0

    lax.fori_loop(0, 2 * mem, finish, 0, unroll=4)


def body(nz, nm, perturbations, zonal_rate, meridional_rate, amplitude):
    mem = perturbations.shape[1]
    rows = 16 * mem
    vmem = pltpu.VMEM
    split1, split2 = 12, 24
    return pl.pallas_call(
        functools.partial(kernel, nz, nm, mem, split1, split2),
        out_shape=jax.ShapeDtypeStruct(perturbations.shape, F32),
        in_specs=[
            pl.BlockSpec(memory_space=pl.ANY),
            pl.BlockSpec(memory_space=pltpu.VMEM),
            pl.BlockSpec(memory_space=pltpu.VMEM),
            pl.BlockSpec(memory_space=pl.ANY),
        ],
        out_specs=pl.BlockSpec(memory_space=pltpu.VMEM),
        scratch_shapes=[
            vmem((2, mem, 128, 128), F32),
            vmem((2, 2, 128, 128), F32),
            vmem((4, mem, 128, 128), F32),
            vmem((16, 128), F32), vmem((16, 128), F32),
            vmem((16, 128), F32), vmem((16, 128), F32),
            vmem((2, 256, 256), BF16), vmem((2, 256, 128), BF16),
            vmem((4, 128, 256), BF16), vmem((4, 128, 128), BF16),
            *[vmem((rows, 128), F32) for _ in range(8)],
            vmem((4, 1, 128), F32), vmem((nz, 1, 128), F32),
            vmem((8, 128), F32), vmem((8 * nm, 128), F32),
            vmem((8, 128), F32), vmem((8 * nm, 128), F32),
            vmem((8, nm, 128), F32),
            vmem((rows, 128), F32), vmem((rows, 128), F32), vmem((16, 256), F32),
            pltpu.SemaphoreType.DMA((2,)),
            pltpu.SemaphoreType.DMA((7,)),
            pltpu.SemaphoreType.DMA((7,)),
        ],
        compiler_params=pltpu.CompilerParams(
            collective_id=0, has_side_effects=True, vmem_limit_bytes=48 * 1024 * 1024
        ),
    )(perturbations, zonal_rate, meridional_rate, amplitude)


def solution(mesh):
    spec = P(None, None, "lat", "lon")
    return jax.shard_map(
        functools.partial(body, mesh.shape["lon"], mesh.shape["lat"]),
        mesh=mesh,
        in_specs=(spec, P(None, None, "lon"), P(), spec),
        out_specs=spec,
        check_vma=False,
    )
```

```python
import functools

import jax
import jax.numpy as jnp
from jax import lax
from jax.experimental import pallas as pl
from jax.experimental.pallas import tpu as pltpu
from jax.sharding import PartitionSpec as P

MESH = pl.DeviceIdType.MESH
F32, BF16 = jnp.float32, jnp.bfloat16
HIGHEST = lax.Precision.HIGHEST

NN = (((1,), (0,)), ((), ()))
NT = (((1,), (1,)), ((), ()))
TN = (((0,), (0,)), ((), ()))


def halves(x):
    high = x.astype(BF16)
    return high, (x - high.astype(F32)).astype(BF16)


def mul(a, b, dims):
    return lax.dot_general(a, b, dims, preferred_element_type=F32)


def dot3(a, b, dims):
    ah, al = halves(a)
    bh, bl = halves(b)
    ka, kb = dims[0][0][0], dims[0][1][0]
    return mul(jnp.concatenate([ah, al], ka), jnp.concatenate([bh, bh], kb), dims) + mul(
        ah, bl, dims
    )


def lane(shape):
    return lax.broadcasted_iota(jnp.int32, shape, 1)


def row(shape):
    return lax.broadcasted_iota(jnp.int32, shape, 0)


def scan_lanes(v, steps, sign):
    width = v.shape[1]
    for k, factor in steps:
        v = v + factor * pltpu.roll(v, k if sign > 0 else width - k, 1)
    return v


def solve(states, coupling, blocks, cyclic):
    g, r, e1e2, w1e2, e1w2, w1w2 = coupling
    shape = (blocks, 128)
    at = row(shape)
    levels = blocks.bit_length() - 1

    def shifted(x, k):
        moved = pltpu.roll(x, k % blocks, 0)
        if cyclic:
            return moved
        return jnp.where((at >= k) if k > 0 else (at < blocks + k), moved, 0.0)

    factors = {}
    for sign in (1, -1):
        a = pltpu.roll(g, sign % blocks, 0)
        factors[sign] = []
        for level in range(levels):
            factors[sign].append(a)
            a = a * pltpu.roll(a, (sign * 2**level) % blocks, 0)
        factors[sign].append(1.0 / (1.0 - a) if cyclic else None)

    def carry(parts, sign):
        out = []
        for v in parts:
            v = shifted(v, sign)
            for level in range(levels):
                v = v + factors[sign][level] * shifted(v, sign * 2**level)
            out.append(v * factors[sign][levels] if cyclic else v)
        return out

    n = len(states[0])
    e1 = carry(states[0], 1)
    w1 = carry([states[1][i] + r * e1[i] for i in range(n)], -1)
    e2 = carry([states[2][i] + e1e2 * e1[i] + w1e2 * w1[i] for i in range(n)], 1)
    w2 = carry(
        [states[3][i] + e1w2 * e1[i] + w1w2 * w1[i] + r * e2[i] for i in range(n)], -1
    )
    return e1, w1, e2, w2


def kernel(
    nz, nm, mem, split1, split2,
    x_hbm, zr_hbm, mr_hbm, amp_hbm, out_ref,
    x_ref, zr_ref, mr_ref, amp_ref, field,
    vz_ref, vm_ref, uz_ref, um_ref,
    az_wide, az_low, am_wide, am_low,
    qs, qr, rs, rin, ps, pr, prs, pin,
    kz_own, kz_all, km_own, km_all, crs, crr, centre,
    lq_ref, d_ref, cr_tile,
    load_sem, send_sem, recv_sem,
):
    zi, mi = lax.axis_index("lon"), lax.axis_index("lat")
    rows = 16 * mem
    zrows, mrows = rows // nz, rows // nm
    per_pair = 4 * mem

    barrier = pltpu.get_barrier_semaphore()

    def greet_lon(k, _):
        pl.semaphore_signal(
            barrier, inc=1, device_id={"lon": lax.rem(zi + k, nz)}, device_id_type=MESH
        )
        return 0

    def greet_lat(k, _):
        pl.semaphore_signal(
            barrier, inc=1, device_id={"lat": lax.rem(mi + k, nm)}, device_id_type=MESH
        )
        return 0

    own = pl.ds(pl.multiple_of(mi * 128, 128), 128)
    zr_copy = pltpu.make_async_copy(zr_hbm, zr_ref, load_sem.at[2])
    mr_copy = pltpu.make_async_copy(mr_hbm.at[:, :, own], mr_ref, load_sem.at[3])
    x_copy = pltpu.make_async_copy(x_hbm, x_ref, load_sem.at[0])
    amp_copy = pltpu.make_async_copy(amp_hbm, amp_ref, load_sem.at[1])
    zr_copy.start()
    mr_copy.start()
    x_copy.start()
    amp_copy.start()
    lax.fori_loop(1, nz, greet_lon, 0)
    lax.fori_loop(1, nm, greet_lat, 0)

    zr_copy.wait()
    mr_copy.wait()
    a = jnp.concatenate([zr_ref[0], zr_ref[1], mr_ref[0], mr_ref[1]], axis=0)
    loss = 1.0 - a
    la = jnp.log(a)
    square = (128, 128)
    upto = jnp.where(row(square) <= lane(square), 1.0, 0.0)
    li = lax.dot_general(la, upto, NN, precision=HIGHEST, preferred_element_type=F32)
    lx = li - la
    total = li[:, 127:128]
    at = lane((8, 128))
    east_cols, west_cols, east_rows, west_rows = [], [], [], []
    for p in range(7):
        k = 2**p
        back = pltpu.roll(li, k, 1)
        ahead = pltpu.roll(li, 128 - k, 1)
        xback = pltpu.roll(lx, k, 1)
        xahead = pltpu.roll(lx, 128 - k, 1)
        first, last = at >= k, at < 128 - k
        east_cols.append((k, jnp.where(first, jnp.exp(jnp.where(first, li - back, 0.0)), 0.0)))
        east_rows.append((k, jnp.where(last, jnp.exp(jnp.where(last, ahead - li, 0.0)), 0.0)))
        west_cols.append((k, jnp.where(last, jnp.exp(jnp.where(last, xahead - lx, 0.0)), 0.0)))
        west_rows.append((k, jnp.where(first, jnp.exp(jnp.where(first, lx - xback, 0.0)), 0.0)))

    def rows_east(v):
        return loss * scan_lanes(v, east_rows, -1)

    def rows_west(v):
        return loss * scan_lanes(v, west_rows, 1)

    def cols_east(x):
        return scan_lanes(loss * x, east_cols, 1)

    def cols_west(x):
        return scan_lanes(loss * x, west_cols, -1)

    ge = jnp.exp(li)
    gw = jnp.exp(total - lx)
    v1 = jnp.exp(total - li) * loss
    w0 = jnp.exp(lx) * loss
    v2 = rows_east(w0)
    x1 = rows_west(v1)
    v3 = rows_east(x1)
    x2 = rows_west(v2)
    v4 = rows_east(x2)

    def along(v):
        return jnp.sum(v, axis=1, keepdims=True)

    kinds = (
        jnp.exp(total), along(w0 * ge), along(x1 * ge),
        along(v1 * gw), along(x2 * ge), along(v2 * gw),
    )
    packed = jnp.zeros((8, 128), F32)
    for k, value in enumerate(kinds):
        packed = jnp.where(at == k, value, packed)
    for n in range(4):
        kz_own[n] = packed[n : n + 1]
    km_own[0:4] = packed[4:8]
    km_own[4:8] = packed[4:8]
    for f, v in enumerate((v1, v2, v3, v4)):
        for n in range(4):
            vz_ref[n * 4 + f : n * 4 + f + 1, :] = v[n : n + 1]
            vm_ref[n * 4 + f : n * 4 + f + 1, :] = v[4 + n : 5 + n]

    x_copy.wait()
    for l in range(2):
        both = [
            jnp.concatenate([ref[l * 4 : l * 4 + 4], ref[8 + l * 4 : 12 + l * 4]], axis=0)
            for ref in (vz_ref, vm_ref)
        ]
        zh, zl = halves(both[0])
        mh, ml = halves(both[1])
        z_wide = jnp.concatenate([zh, zl], axis=1)
        m_wide = jnp.concatenate([mh, ml], axis=1)

        def states(m, _):
            xh, xl = halves(x_ref[l, m])
            q = mul(z_wide, jnp.concatenate([xh, xh], axis=1), NT) + mul(zh, xl, NT)
            p = mul(m_wide, jnp.concatenate([xh, xh], axis=0), NN) + mul(mh, xl, NN)
            for s in range(2):
                base = (s * 2 + l) * per_pair
                qs[pl.ds(base + m * 4, 4), :] = q[s * 4 : s * 4 + 4]
                ps[pl.ds(base + m * 4, 4), :] = p[s * 4 : s * 4 + 4]
            return 0

        lax.fori_loop(0, mem, states, 0, unroll=4)

    pl.semaphore_wait(barrier, nz + nm - 2)

    def chunk(ref, index, size):
        return ref.at[pl.ds(pl.multiple_of(index * size, size), size), :]

    def remote(src, dst, which, **device):
        return pltpu.make_async_remote_copy(
            src_ref=src, dst_ref=dst,
            send_sem=send_sem.at[which], recv_sem=recv_sem.at[which],
            device_id=device, device_id_type=MESH,
        )

    other_z, other_m = lax.rem(zi + 1, nz), lax.rem(mi + 1, nm)

    def send_lon(k, _):
        d = lax.rem(zi + k, nz)
        remote(kz_own.at[d * zrows // per_pair], kz_all.at[zi], 1, lon=d).start()
        remote(chunk(qs, d, zrows), chunk(qr, zi, zrows), 0, lon=d).start()
        return 0

    def send_lat(k, _):
        d = lax.rem(mi + k, nm)
        remote(chunk(ps, d, mrows), chunk(pr, mi, mrows), 2, lat=d).start()
        remote(km_own, chunk(km_all, mi, 8), 3, lat=d).start()
        return 0

    lax.fori_loop(1, nz, send_lon, 0)
    lax.fori_loop(1, nm, send_lat, 0)
    kz_all[zi] = kz_own[zi * zrows // per_pair]
    chunk(qr, zi, zrows)[...] = chunk(qs, zi, zrows)[...]
    chunk(pr, mi, mrows)[...] = chunk(ps, mi, mrows)[...]
    chunk(km_all, mi, 8)[...] = km_own[...]

    u3 = cols_west(ge)
    u2 = cols_west(cols_east(gw))
    u1 = cols_west(cols_east(u3))
    for f, u in enumerate((u1, u2, u3, gw)):
        for n in range(4):
            uz_ref[n * 4 + f : n * 4 + f + 1, :] = u[n : n + 1]
            um_ref[n * 4 + f : n * 4 + f + 1, :] = u[4 + n : 5 + n]

    lit, lxt = jnp.transpose(li), jnp.transpose(lx)
    below = row(square) >= lane(square)
    above = row(square) <= lane(square)
    for n in range(8):
        down = jnp.where(below, lit[:, n : n + 1] - li[n : n + 1], 0.0)
        up = jnp.where(above, lx[n : n + 1] - lxt[:, n : n + 1], 0.0)
        east = jnp.where(below, jnp.exp(down), 0.0) * loss[n : n + 1]
        west = jnp.where(above, jnp.exp(up), 0.0) * loss[n : n + 1]
        once = dot3(west, east, NN)
        high, low = halves(dot3(once, once, NN))
        if n < 4:
            s, l = n // 2, n % 2
            az_wide[l, s * 128 : s * 128 + 128, 0:128] = high
            az_wide[l, s * 128 : s * 128 + 128, 128:256] = high
            az_low[l, s * 128 : s * 128 + 128, :] = low
        else:
            am_wide[n - 4, :, 0:128] = high
            am_wide[n - 4, :, 128:256] = high
            am_low[n - 4] = low

    def local_pass(i, _):
        l, m = i // mem, lax.rem(i, mem)
        xh, xl = halves(x_ref[l, m])
        f = mul(jnp.concatenate([xh, xl], axis=1), az_wide[l], NT) + mul(xh, az_low[l], NT)
        for s in range(2):
            n = s * 2 + l
            fh, fl = halves(f[:, s * 128 : s * 128 + 128])
            field[n, m] = mul(am_wide[n], jnp.concatenate([fh, fl], axis=0), NN) + mul(
                am_low[n], fh, NN
            )
        return 0

    lax.fori_loop(0, split1, local_pass, 0, unroll=2)

    zshape, mshape = (nz, 128), (nm, 128)
    remote(qs.at[pl.ds(0, (nz - 1) * zrows)], qr.at[pl.ds(0, (nz - 1) * zrows)], 0, lon=other_z).wait()
    remote(kz_all.at[pl.ds(0, nz - 1)], kz_all.at[pl.ds(0, nz - 1)], 1, lon=other_z).wait()
    kz = kz_all[...].reshape(nz, 128)
    coupling = [jnp.broadcast_to(kz[:, k : k + 1], zshape) for k in range(6)]
    groups = zrows // 4
    got = [
        [qr[pl.ds(g * 4 + f, nz, stride=zrows), :] for g in range(groups)] for f in range(4)
    ]
    for f, parts in enumerate(solve(got, coupling, nz, True)):
        for g in range(groups):
            rs[pl.ds(g * 4 + f, nz, stride=zrows), :] = parts[g]

    def back_lon(k, _):
        d = lax.rem(zi + k, nz)
        remote(chunk(rs, d, zrows), chunk(rin, zi, zrows), 4, lon=d).start()
        return 0

    lax.fori_loop(1, nz, back_lon, 0)
    chunk(rin, zi, zrows)[...] = chunk(rs, zi, zrows)[...]

    remote(ps.at[pl.ds(0, (nm - 1) * mrows)], pr.at[pl.ds(0, (nm - 1) * mrows)], 2, lat=other_m).wait()
    remote(km_all.at[pl.ds(0, (nm - 1) * 8)], km_all.at[pl.ds(0, (nm - 1) * 8)], 3, lat=other_m).wait()
    pair = mi * mrows // per_pair
    km = [km_all[pl.ds(n, nm, stride=8), :] for n in range(4)]
    mine = km[0]
    for n in range(1, 4):
        mine = jnp.where(pair == n, km[n], mine)
    coupling = [jnp.broadcast_to(mine[:, k : k + 1], mshape) for k in range(6)]
    groups = mrows // 4
    got = [
        [pr[pl.ds(g * 4 + f, nm, stride=mrows), :] for g in range(groups)] for f in range(4)
    ]
    for f, parts in enumerate(solve(got, coupling, nm, False)):
        for g in range(groups):
            prs[pl.ds(g * 4 + f, nm, stride=mrows), :] = parts[g]

    def back_lat(k, _):
        d = lax.rem(mi + k, nm)
        remote(chunk(prs, d, mrows), chunk(pin, mi, mrows), 5, lat=d).start()
        return 0

    lax.fori_loop(1, nm, back_lat, 0)
    chunk(pin, mi, mrows)[...] = chunk(prs, mi, mrows)[...]

    lax.fori_loop(split1, split2, local_pass, 0, unroll=2)

    remote(rs.at[pl.ds(0, (nz - 1) * zrows)], rin.at[pl.ds(0, (nz - 1) * zrows)], 4, lon=other_z).wait()
    cross = dot3(vm_ref[...], rin[...], NT)
    wide = (16, rows)
    cross = jnp.where(row(wide) // 4 == lane(wide) // per_pair, cross, 0.0)
    cross = cross[0:4] + cross[4:8] + cross[8:12] + cross[12:16]
    crs[0:4] = cross[:, 0:128]
    crs[4:8] = cross[:, 128:256]

    def send_cross(k, _):
        d = lax.rem(mi + k, nm)
        remote(crs, chunk(crr, mi, 8), 6, lat=d).start()
        return 0

    lax.fori_loop(1, nm, send_cross, 0)
    chunk(crr, mi, 8)[...] = crs[...]

    lax.fori_loop(split2, 2 * mem, local_pass, 0, unroll=2)

    remote(prs.at[pl.ds(0, (nm - 1) * mrows)], pin.at[pl.ds(0, (nm - 1) * mrows)], 5, lat=other_m).wait()
    for n in range(4):
        s, l = n // 2, n % 2
        part = slice(n * per_pair, (n + 1) * per_pair)
        ph, plow = halves(pin[part])
        d_ref[part] = mul(
            jnp.concatenate([ph, plow], axis=1), az_wide[l, s * 128 : s * 128 + 128, :], NT
        ) + mul(ph, az_low[l, s * 128 : s * 128 + 128, :], NT)
        qh, ql = halves(rin[part])
        lq_ref[part] = mul(jnp.concatenate([qh, ql], axis=1), am_wide[n], NT) + mul(
            qh, am_low[n], NT
        )
    amp_copy.wait()

    remote(crr.at[pl.ds(0, (nm - 1) * 8)], crr.at[pl.ds(0, (nm - 1) * 8)], 6, lat=other_m).wait()
    for h in range(2):
        left = lane(mshape) < per_pair
        coupling = [
            jnp.where(left, km[2 * h][:, k : k + 1], km[2 * h + 1][:, k : k + 1])
            for k in range(6)
        ]
        got = [[crr[pl.ds(h * 4 + f, nm, stride=8), :]] for f in range(4)]
        for f, parts in enumerate(solve(got, coupling, nm, False)):
            centre[h * 4 + f] = parts[0]
    for n in range(4):
        h = n // 2
        for f in range(4):
            line = centre[h * 4 + f, pl.ds(mi, 1), :]
            line = jnp.where(lane((1, 128)) // per_pair == n % 2, line, 0.0)
            r = n * 4 + f
            cr_tile[r : r + 1, h * 128 : h * 128 + 128] = line
            cr_tile[r : r + 1, (1 - h) * 128 : (1 - h) * 128 + 128] = jnp.zeros((1, 128), F32)
    lq_ref[...] += dot3(cr_tile[...], um_ref[...], TN)

    def finish(i, _):
        l, m = i // mem, lax.rem(i, mem)
        result = None
        for s in range(2):
            n = s * 2 + l
            part = pl.ds(n * per_pair + m * 4, 4)
            resp = pl.ds(n * 4, 4)
            left = jnp.concatenate([lq_ref[part, :], um_ref[resp, :]], axis=0)
            right = jnp.concatenate([uz_ref[resp, :], d_ref[part, :]], axis=0)
            lh = left.astype(BF16).astype(F32)
            rh = right.astype(BF16).astype(F32)
            stacked_left = jnp.concatenate([lh, left - lh, lh], axis=0).astype(BF16)
            stacked_right = jnp.concatenate([rh, rh, right - rh], axis=0).astype(BF16)
            y = field[n, m] + mul(stacked_left, stacked_right, TN)
            y = y * amp_ref[s, l]
            result = y if result is None else result + y
        out_ref[l, m] = result
        return 0

    lax.fori_loop(0, 2 * mem, finish, 0, unroll=4)


def body(nz, nm, perturbations, zonal_rate, meridional_rate, amplitude):
    mem = perturbations.shape[1]
    rows = 16 * mem
    vmem = pltpu.VMEM
    split1, split2 = 12, 24
    return pl.pallas_call(
        functools.partial(kernel, nz, nm, mem, split1, split2),
        out_shape=jax.ShapeDtypeStruct(perturbations.shape, F32),
        in_specs=[
            pl.BlockSpec(memory_space=pltpu.HBM) for _ in range(4)
        ],
        out_specs=pl.BlockSpec(memory_space=pltpu.VMEM),
        scratch_shapes=[
            vmem((2, mem, 128, 128), F32),
            vmem((2, 2, 128), F32), vmem((2, 2, 128), F32),
            vmem((2, 2, 128, 128), F32),
            vmem((4, mem, 128, 128), F32),
            vmem((16, 128), F32), vmem((16, 128), F32),
            vmem((16, 128), F32), vmem((16, 128), F32),
            vmem((2, 256, 256), BF16), vmem((2, 256, 128), BF16),
            vmem((4, 128, 256), BF16), vmem((4, 128, 128), BF16),
            *[vmem((rows, 128), F32) for _ in range(8)],
            vmem((4, 1, 128), F32), vmem((nz, 1, 128), F32),
            vmem((8, 128), F32), vmem((8 * nm, 128), F32),
            vmem((8, 128), F32), vmem((8 * nm, 128), F32),
            vmem((8, nm, 128), F32),
            vmem((rows, 128), F32), vmem((rows, 128), F32), vmem((16, 256), F32),
            pltpu.SemaphoreType.DMA((4,)),
            pltpu.SemaphoreType.DMA((7,)),
            pltpu.SemaphoreType.DMA((7,)),
        ],
        compiler_params=pltpu.CompilerParams(
            collective_id=0, has_side_effects=True, vmem_limit_bytes=48 * 1024 * 1024
        ),
    )(*(pltpu.with_memory_space_constraint(v, pltpu.HBM) for v in (perturbations, zonal_rate, meridional_rate, amplitude)))


def solution(mesh):
    spec = P(None, None, "lat", "lon")
    return jax.shard_map(
        functools.partial(body, mesh.shape["lon"], mesh.shape["lat"]),
        mesh=mesh,
        in_specs=(spec, P(None, None, "lon"), P(), spec),
        out_specs=spec,
        check_vma=False,
    )
```

```python
import functools

import jax
import jax.numpy as jnp
from jax import lax
from jax.experimental import pallas as pl
from jax.experimental.pallas import tpu as pltpu
from jax.sharding import PartitionSpec as P

MESH = pl.DeviceIdType.MESH
F32, BF16 = jnp.float32, jnp.bfloat16
HIGHEST = lax.Precision.HIGHEST

NN = (((1,), (0,)), ((), ()))
NT = (((1,), (1,)), ((), ()))
TN = (((0,), (0,)), ((), ()))


def halves(x):
    high = x.astype(BF16)
    return high, (x - high.astype(F32)).astype(BF16)


def mul(a, b, dims):
    return lax.dot_general(a, b, dims, preferred_element_type=F32)


def dot3(a, b, dims):
    ah, al = halves(a)
    bh, bl = halves(b)
    ka, kb = dims[0][0][0], dims[0][1][0]
    return mul(jnp.concatenate([ah, al], ka), jnp.concatenate([bh, bh], kb), dims) + mul(
        ah, bl, dims
    )


def lane(shape):
    return lax.broadcasted_iota(jnp.int32, shape, 1)


def row(shape):
    return lax.broadcasted_iota(jnp.int32, shape, 0)


def scan_lanes(v, steps, sign):
    width = v.shape[1]
    for k, factor in steps:
        v = v + factor * pltpu.roll(v, k if sign > 0 else width - k, 1)
    return v


def solve(states, coupling, blocks, cyclic):
    g, r, e1e2, w1e2, e1w2, w1w2 = coupling
    shape = (blocks, 128)
    at = row(shape)
    levels = blocks.bit_length() - 1

    def shifted(x, k):
        moved = pltpu.roll(x, k % blocks, 0)
        if cyclic:
            return moved
        return jnp.where((at >= k) if k > 0 else (at < blocks + k), moved, 0.0)

    factors = {}
    for sign in (1, -1):
        a = pltpu.roll(g, sign % blocks, 0)
        factors[sign] = []
        for level in range(levels):
            factors[sign].append(a)
            a = a * pltpu.roll(a, (sign * 2**level) % blocks, 0)
        factors[sign].append(1.0 / (1.0 - a) if cyclic else None)

    def carry(parts, sign):
        out = []
        for v in parts:
            v = shifted(v, sign)
            for level in range(levels):
                v = v + factors[sign][level] * shifted(v, sign * 2**level)
            out.append(v * factors[sign][levels] if cyclic else v)
        return out

    n = len(states[0])
    e1 = carry(states[0], 1)
    w1 = carry([states[1][i] + r * e1[i] for i in range(n)], -1)
    e2 = carry([states[2][i] + e1e2 * e1[i] + w1e2 * w1[i] for i in range(n)], 1)
    w2 = carry(
        [states[3][i] + e1w2 * e1[i] + w1w2 * w1[i] + r * e2[i] for i in range(n)], -1
    )
    return e1, w1, e2, w2


def kernel(
    nz, nm, mem, split1, split2,
    x_hbm, zr_hbm, mr_hbm, amp_hbm, out_ref,
    x_ref, zr_ref, mr_ref, amp_ref, field,
    vz_ref, vm_ref, uz_ref, um_ref,
    az_wide, az_low, am_wide, am_low,
    qs, qr, rs, rin, ps, pr, prs, pin,
    kz_own, kz_all, km_own, km_all, crs, crr, centre,
    lq_ref, d_ref, cr_tile,
    load_sem, send_sem, recv_sem,
):
    zi, mi = lax.axis_index("lon"), lax.axis_index("lat")
    rows = 16 * mem
    zrows, mrows = rows // nz, rows // nm
    per_pair = 4 * mem

    barrier = pltpu.get_barrier_semaphore()

    def greet_lon(k, _):
        pl.semaphore_signal(
            barrier, inc=1, device_id={"lon": lax.rem(zi + k, nz)}, device_id_type=MESH
        )
        return 0

    def greet_lat(k, _):
        pl.semaphore_signal(
            barrier, inc=1, device_id={"lat": lax.rem(mi + k, nm)}, device_id_type=MESH
        )
        return 0

    own = pl.ds(pl.multiple_of(mi * 128, 128), 128)
    zr_copy = pltpu.make_async_copy(zr_hbm, zr_ref, load_sem.at[2])
    mr_copy = pltpu.make_async_copy(mr_hbm.at[:, :, own], mr_ref, load_sem.at[3])
    x_copy = pltpu.make_async_copy(x_hbm, x_ref, load_sem.at[0])
    amp_copy = pltpu.make_async_copy(amp_hbm, amp_ref, load_sem.at[1])
    zr_copy.start()
    mr_copy.start()
    x_copy.start()
    amp_copy.start()
    lax.fori_loop(1, nz, greet_lon, 0)
    lax.fori_loop(1, nm, greet_lat, 0)

    zr_copy.wait()
    mr_copy.wait()
    a = jnp.concatenate([zr_ref[0], zr_ref[1], mr_ref[0], mr_ref[1]], axis=0)
    loss = 1.0 - a
    la = jnp.log(a)
    square = (128, 128)
    upto = jnp.where(row(square) <= lane(square), 1.0, 0.0)
    li = lax.dot_general(la, upto, NN, precision=HIGHEST, preferred_element_type=F32)
    lx = li - la
    total = li[:, 127:128]
    at = lane((8, 128))
    east_cols, west_cols, east_rows, west_rows = [], [], [], []
    for p in range(7):
        k = 2**p
        back = pltpu.roll(li, k, 1)
        ahead = pltpu.roll(li, 128 - k, 1)
        xback = pltpu.roll(lx, k, 1)
        xahead = pltpu.roll(lx, 128 - k, 1)
        first, last = at >= k, at < 128 - k
        east_cols.append((k, jnp.where(first, jnp.exp(jnp.where(first, li - back, 0.0)), 0.0)))
        east_rows.append((k, jnp.where(last, jnp.exp(jnp.where(last, ahead - li, 0.0)), 0.0)))
        west_cols.append((k, jnp.where(last, jnp.exp(jnp.where(last, xahead - lx, 0.0)), 0.0)))
        west_rows.append((k, jnp.where(first, jnp.exp(jnp.where(first, lx - xback, 0.0)), 0.0)))

    def rows_east(v):
        return loss * scan_lanes(v, east_rows, -1)

    def rows_west(v):
        return loss * scan_lanes(v, west_rows, 1)

    def cols_east(x):
        return scan_lanes(loss * x, east_cols, 1)

    def cols_west(x):
        return scan_lanes(loss * x, west_cols, -1)

    ge = jnp.exp(li)
    gw = jnp.exp(total - lx)
    v1 = jnp.exp(total - li) * loss
    w0 = jnp.exp(lx) * loss
    v2 = rows_east(w0)
    x1 = rows_west(v1)
    v3 = rows_east(x1)
    x2 = rows_west(v2)
    v4 = rows_east(x2)

    def along(v):
        return jnp.sum(v, axis=1, keepdims=True)

    kinds = (
        jnp.exp(total), along(w0 * ge), along(x1 * ge),
        along(v1 * gw), along(x2 * ge), along(v2 * gw),
    )
    packed = jnp.zeros((8, 128), F32)
    for k, value in enumerate(kinds):
        packed = jnp.where(at == k, value, packed)
    for n in range(4):
        kz_own[n] = packed[n : n + 1]
    km_own[0:4] = packed[4:8]
    km_own[4:8] = packed[4:8]
    for f, v in enumerate((v1, v2, v3, v4)):
        for n in range(4):
            vz_ref[n * 4 + f : n * 4 + f + 1, :] = v[n : n + 1]
            vm_ref[n * 4 + f : n * 4 + f + 1, :] = v[4 + n : 5 + n]

    x_copy.wait()
    for l in range(2):
        both = [
            jnp.concatenate([ref[l * 4 : l * 4 + 4], ref[8 + l * 4 : 12 + l * 4]], axis=0)
            for ref in (vz_ref, vm_ref)
        ]
        zh, zl = halves(both[0])
        mh, ml = halves(both[1])
        z_wide = jnp.concatenate([zh, zl], axis=1)
        m_wide = jnp.concatenate([mh, ml], axis=1)

        def states(m, _):
            xh, xl = halves(x_ref[l, m])
            q = mul(z_wide, jnp.concatenate([xh, xh], axis=1), NT) + mul(zh, xl, NT)
            p = mul(m_wide, jnp.concatenate([xh, xh], axis=0), NN) + mul(mh, xl, NN)
            for s in range(2):
                base = (s * 2 + l) * per_pair
                qs[pl.ds(base + m * 4, 4), :] = q[s * 4 : s * 4 + 4]
                ps[pl.ds(base + m * 4, 4), :] = p[s * 4 : s * 4 + 4]
            return 0

        lax.fori_loop(0, mem, states, 0, unroll=16)

    pl.semaphore_wait(barrier, nz + nm - 2)

    def chunk(ref, index, size):
        return ref.at[pl.ds(pl.multiple_of(index * size, size), size), :]

    def remote(src, dst, which, **device):
        return pltpu.make_async_remote_copy(
            src_ref=src, dst_ref=dst,
            send_sem=send_sem.at[which], recv_sem=recv_sem.at[which],
            device_id=device, device_id_type=MESH,
        )

    other_z, other_m = lax.rem(zi + 1, nz), lax.rem(mi + 1, nm)

    def send_lon(k, _):
        d = lax.rem(zi + k, nz)
        remote(kz_own.at[d * zrows // per_pair], kz_all.at[zi], 1, lon=d).start()
        remote(chunk(qs, d, zrows), chunk(qr, zi, zrows), 0, lon=d).start()
        return 0

    def send_lat(k, _):
        d = lax.rem(mi + k, nm)
        remote(chunk(ps, d, mrows), chunk(pr, mi, mrows), 2, lat=d).start()
        remote(km_own, chunk(km_all, mi, 8), 3, lat=d).start()
        return 0

    lax.fori_loop(1, nz, send_lon, 0)
    lax.fori_loop(1, nm, send_lat, 0)
    kz_all[zi] = kz_own[zi * zrows // per_pair]
    chunk(qr, zi, zrows)[...] = chunk(qs, zi, zrows)[...]
    chunk(pr, mi, mrows)[...] = chunk(ps, mi, mrows)[...]
    chunk(km_all, mi, 8)[...] = km_own[...]

    u3 = cols_west(ge)
    u2 = cols_west(cols_east(gw))
    u1 = cols_west(cols_east(u3))
    for f, u in enumerate((u1, u2, u3, gw)):
        for n in range(4):
            uz_ref[n * 4 + f : n * 4 + f + 1, :] = u[n : n + 1]
            um_ref[n * 4 + f : n * 4 + f + 1, :] = u[4 + n : 5 + n]

    lit, lxt = jnp.transpose(li), jnp.transpose(lx)
    below = row(square) >= lane(square)
    above = row(square) <= lane(square)
    for n in range(8):
        down = jnp.where(below, lit[:, n : n + 1] - li[n : n + 1], 0.0)
        up = jnp.where(above, lx[n : n + 1] - lxt[:, n : n + 1], 0.0)
        east = jnp.where(below, jnp.exp(down), 0.0) * loss[n : n + 1]
        west = jnp.where(above, jnp.exp(up), 0.0) * loss[n : n + 1]
        once = dot3(west, east, NN)
        high, low = halves(dot3(once, once, NN))
        if n < 4:
            s, l = n // 2, n % 2
            az_wide[l, s * 128 : s * 128 + 128, 0:128] = high
            az_wide[l, s * 128 : s * 128 + 128, 128:256] = high
            az_low[l, s * 128 : s * 128 + 128, :] = low
        else:
            am_wide[n - 4, :, 0:128] = high
            am_wide[n - 4, :, 128:256] = high
            am_low[n - 4] = low

    def local_pass(i, _):
        l, m = i // mem, lax.rem(i, mem)
        xh, xl = halves(x_ref[l, m])
        f = mul(jnp.concatenate([xh, xl], axis=1), az_wide[l], NT) + mul(xh, az_low[l], NT)
        for s in range(2):
            n = s * 2 + l
            fh, fl = halves(f[:, s * 128 : s * 128 + 128])
            field[n, m] = mul(am_wide[n], jnp.concatenate([fh, fl], axis=0), NN) + mul(
                am_low[n], fh, NN
            )
        return 0

    lax.fori_loop(0, split1, local_pass, 0, unroll=8)

    zshape, mshape = (nz, 128), (nm, 128)
    remote(qs.at[pl.ds(0, (nz - 1) * zrows)], qr.at[pl.ds(0, (nz - 1) * zrows)], 0, lon=other_z).wait()
    remote(kz_all.at[pl.ds(0, nz - 1)], kz_all.at[pl.ds(0, nz - 1)], 1, lon=other_z).wait()
    kz = kz_all[...].reshape(nz, 128)
    coupling = [jnp.broadcast_to(kz[:, k : k + 1], zshape) for k in range(6)]
    groups = zrows // 4
    got = [
        [qr[pl.ds(g * 4 + f, nz, stride=zrows), :] for g in range(groups)] for f in range(4)
    ]
    for f, parts in enumerate(solve(got, coupling, nz, True)):
        for g in range(groups):
            rs[pl.ds(g * 4 + f, nz, stride=zrows), :] = parts[g]

    def back_lon(k, _):
        d = lax.rem(zi + k, nz)
        remote(chunk(rs, d, zrows), chunk(rin, zi, zrows), 4, lon=d).start()
        return 0

    lax.fori_loop(1, nz, back_lon, 0)
    chunk(rin, zi, zrows)[...] = chunk(rs, zi, zrows)[...]

    remote(ps.at[pl.ds(0, (nm - 1) * mrows)], pr.at[pl.ds(0, (nm - 1) * mrows)], 2, lat=other_m).wait()
    remote(km_all.at[pl.ds(0, (nm - 1) * 8)], km_all.at[pl.ds(0, (nm - 1) * 8)], 3, lat=other_m).wait()
    pair = mi * mrows // per_pair
    km = [km_all[pl.ds(n, nm, stride=8), :] for n in range(4)]
    mine = km[0]
    for n in range(1, 4):
        mine = jnp.where(pair == n, km[n], mine)
    coupling = [jnp.broadcast_to(mine[:, k : k + 1], mshape) for k in range(6)]
    groups = mrows // 4
    got = [
        [pr[pl.ds(g * 4 + f, nm, stride=mrows), :] for g in range(groups)] for f in range(4)
    ]
    for f, parts in enumerate(solve(got, coupling, nm, False)):
        for g in range(groups):
            prs[pl.ds(g * 4 + f, nm, stride=mrows), :] = parts[g]

    def back_lat(k, _):
        d = lax.rem(mi + k, nm)
        remote(chunk(prs, d, mrows), chunk(pin, mi, mrows), 5, lat=d).start()
        return 0

    lax.fori_loop(1, nm, back_lat, 0)
    chunk(pin, mi, mrows)[...] = chunk(prs, mi, mrows)[...]

    lax.fori_loop(split1, split2, local_pass, 0, unroll=8)

    remote(rs.at[pl.ds(0, (nz - 1) * zrows)], rin.at[pl.ds(0, (nz - 1) * zrows)], 4, lon=other_z).wait()
    cross = dot3(vm_ref[...], rin[...], NT)
    wide = (16, rows)
    cross = jnp.where(row(wide) // 4 == lane(wide) // per_pair, cross, 0.0)
    cross = cross[0:4] + cross[4:8] + cross[8:12] + cross[12:16]
    crs[0:4] = cross[:, 0:128]
    crs[4:8] = cross[:, 128:256]

    def send_cross(k, _):
        d = lax.rem(mi + k, nm)
        remote(crs, chunk(crr, mi, 8), 6, lat=d).start()
        return 0

    lax.fori_loop(1, nm, send_cross, 0)
    chunk(crr, mi, 8)[...] = crs[...]

    lax.fori_loop(split2, 2 * mem, local_pass, 0, unroll=8)

    remote(prs.at[pl.ds(0, (nm - 1) * mrows)], pin.at[pl.ds(0, (nm - 1) * mrows)], 5, lat=other_m).wait()
    for n in range(4):
        s, l = n // 2, n % 2
        part = slice(n * per_pair, (n + 1) * per_pair)
        ph, plow = halves(pin[part])
        d_ref[part] = mul(
            jnp.concatenate([ph, plow], axis=1), az_wide[l, s * 128 : s * 128 + 128, :], NT
        ) + mul(ph, az_low[l, s * 128 : s * 128 + 128, :], NT)
        qh, ql = halves(rin[part])
        lq_ref[part] = mul(jnp.concatenate([qh, ql], axis=1), am_wide[n], NT) + mul(
            qh, am_low[n], NT
        )
    amp_copy.wait()

    remote(crr.at[pl.ds(0, (nm - 1) * 8)], crr.at[pl.ds(0, (nm - 1) * 8)], 6, lat=other_m).wait()
    for h in range(2):
        left = lane(mshape) < per_pair
        coupling = [
            jnp.where(left, km[2 * h][:, k : k + 1], km[2 * h + 1][:, k : k + 1])
            for k in range(6)
        ]
        got = [[crr[pl.ds(h * 4 + f, nm, stride=8), :]] for f in range(4)]
        for f, parts in enumerate(solve(got, coupling, nm, False)):
            centre[h * 4 + f] = parts[0]
    for n in range(4):
        h = n // 2
        for f in range(4):
            line = centre[h * 4 + f, pl.ds(mi, 1), :]
            line = jnp.where(lane((1, 128)) // per_pair == n % 2, line, 0.0)
            r = n * 4 + f
            cr_tile[r : r + 1, h * 128 : h * 128 + 128] = line
            cr_tile[r : r + 1, (1 - h) * 128 : (1 - h) * 128 + 128] = jnp.zeros((1, 128), F32)
    lq_ref[...] += dot3(cr_tile[...], um_ref[...], TN)

    def finish(i, _):
        l, m = i // mem, lax.rem(i, mem)
        result = None
        for s in range(2):
            n = s * 2 + l
            part = pl.ds(n * per_pair + m * 4, 4)
            resp = pl.ds(n * 4, 4)
            left = jnp.concatenate([lq_ref[part, :], um_ref[resp, :]], axis=0)
            right = jnp.concatenate([uz_ref[resp, :], d_ref[part, :]], axis=0)
            lh = left.astype(BF16).astype(F32)
            rh = right.astype(BF16).astype(F32)
            stacked_left = jnp.concatenate([lh, left - lh, lh], axis=0).astype(BF16)
            stacked_right = jnp.concatenate([rh, rh, right - rh], axis=0).astype(BF16)
            y = field[n, m] + mul(stacked_left, stacked_right, TN)
            y = y * amp_ref[s, l]
            result = y if result is None else result + y
        out_ref[l, m] = result
        return 0

    lax.fori_loop(0, 2 * mem, finish, 0, unroll=8)


def body(nz, nm, perturbations, zonal_rate, meridional_rate, amplitude):
    mem = perturbations.shape[1]
    rows = 16 * mem
    vmem = pltpu.VMEM
    split1, split2 = 16, 24
    return pl.pallas_call(
        functools.partial(kernel, nz, nm, mem, split1, split2),
        out_shape=jax.ShapeDtypeStruct(perturbations.shape, F32),
        in_specs=[
            pl.BlockSpec(memory_space=pltpu.HBM) for _ in range(4)
        ],
        out_specs=pl.BlockSpec(memory_space=pltpu.VMEM),
        scratch_shapes=[
            vmem((2, mem, 128, 128), F32),
            vmem((2, 2, 128), F32), vmem((2, 2, 128), F32),
            vmem((2, 2, 128, 128), F32),
            vmem((4, mem, 128, 128), F32),
            vmem((16, 128), F32), vmem((16, 128), F32),
            vmem((16, 128), F32), vmem((16, 128), F32),
            vmem((2, 256, 256), BF16), vmem((2, 256, 128), BF16),
            vmem((4, 128, 256), BF16), vmem((4, 128, 128), BF16),
            *[vmem((rows, 128), F32) for _ in range(8)],
            vmem((4, 1, 128), F32), vmem((nz, 1, 128), F32),
            vmem((8, 128), F32), vmem((8 * nm, 128), F32),
            vmem((8, 128), F32), vmem((8 * nm, 128), F32),
            vmem((8, nm, 128), F32),
            vmem((rows, 128), F32), vmem((rows, 128), F32), vmem((16, 256), F32),
            pltpu.SemaphoreType.DMA((4,)),
            pltpu.SemaphoreType.DMA((7,)),
            pltpu.SemaphoreType.DMA((7,)),
        ],
        compiler_params=pltpu.CompilerParams(
            collective_id=0, has_side_effects=True, vmem_limit_bytes=48 * 1024 * 1024
        ),
    )(*(pltpu.with_memory_space_constraint(v, pltpu.HBM) for v in (perturbations, zonal_rate, meridional_rate, amplitude)))


def solution(mesh):
    spec = P(None, None, "lat", "lon")
    return jax.shard_map(
        functools.partial(body, mesh.shape["lon"], mesh.shape["lat"]),
        mesh=mesh,
        in_specs=(spec, P(None, None, "lon"), P(), spec),
        out_specs=spec,
        check_vma=False,
    )
```

```python
import functools

import jax
import jax.numpy as jnp
from jax import lax
from jax.experimental import pallas as pl
from jax.experimental.pallas import tpu as pltpu
from jax.sharding import PartitionSpec as P

MESH = pl.DeviceIdType.MESH
F32, BF16 = jnp.float32, jnp.bfloat16
HIGHEST = lax.Precision.HIGHEST

NN = (((1,), (0,)), ((), ()))
NT = (((1,), (1,)), ((), ()))
TN = (((0,), (0,)), ((), ()))


def halves(x):
    high = x.astype(BF16)
    return high, (x - high.astype(F32)).astype(BF16)


def mul(a, b, dims):
    return lax.dot_general(a, b, dims, preferred_element_type=F32)


def dot3(a, b, dims):
    ah, al = halves(a)
    bh, bl = halves(b)
    ka, kb = dims[0][0][0], dims[0][1][0]
    return mul(jnp.concatenate([ah, al], ka), jnp.concatenate([bh, bh], kb), dims) + mul(
        ah, bl, dims
    )


def lane(shape):
    return lax.broadcasted_iota(jnp.int32, shape, 1)


def row(shape):
    return lax.broadcasted_iota(jnp.int32, shape, 0)


def scan_lanes(v, steps, sign):
    width = v.shape[1]
    for k, factor in steps:
        v = v + factor * pltpu.roll(v, k if sign > 0 else width - k, 1)
    return v


def solve(states, coupling, blocks, cyclic):
    g, r, e1e2, w1e2, e1w2, w1w2 = coupling
    shape = (blocks, 128)
    at = row(shape)
    levels = blocks.bit_length() - 1

    def shifted(x, k):
        moved = pltpu.roll(x, k % blocks, 0)
        if cyclic:
            return moved
        return jnp.where((at >= k) if k > 0 else (at < blocks + k), moved, 0.0)

    factors = {}
    for sign in (1, -1):
        a = pltpu.roll(g, sign % blocks, 0)
        factors[sign] = []
        for level in range(levels):
            factors[sign].append(a)
            a = a * pltpu.roll(a, (sign * 2**level) % blocks, 0)
        factors[sign].append(1.0 / (1.0 - a) if cyclic else None)

    def carry(parts, sign):
        out = []
        for v in parts:
            v = shifted(v, sign)
            for level in range(levels):
                v = v + factors[sign][level] * shifted(v, sign * 2**level)
            out.append(v * factors[sign][levels] if cyclic else v)
        return out

    n = len(states[0])
    e1 = carry(states[0], 1)
    w1 = carry([states[1][i] + r * e1[i] for i in range(n)], -1)
    e2 = carry([states[2][i] + e1e2 * e1[i] + w1e2 * w1[i] for i in range(n)], 1)
    w2 = carry(
        [states[3][i] + e1w2 * e1[i] + w1w2 * w1[i] + r * e2[i] for i in range(n)], -1
    )
    return e1, w1, e2, w2


def kernel(
    nz, nm, mem, lead0, lead1, split1, split2,
    x_hbm, zr_hbm, mr_hbm, amp_hbm,
    field, amp_ref, uz_ref, um_ref, lq_ref, lr_ref, d_ref,
    x_ref, zr_ref, mr_ref, vz_ref, vm_ref,
    az_wide, az_low, am_wide, am_low,
    qs, rin, ps, pr, prs, pin, qr, rs,
    kz_own, kz_all, km_own, km_all, cs_own, cs_all, cz, crs, crr, centre,
    cr_tile,
    load_sem, send_sem, recv_sem,
):
    zi, mi = lax.axis_index("lon"), lax.axis_index("lat")
    rows = 16 * mem
    period = min(nz, 16)
    near, chips, strips = period // 2, period // 2, nz // period
    early_side = lax.rem(zi, period) < near
    zrows, mrows = rows // nz, rows // nm
    z, core, strip = lax.rem(zi, period) // 2, lax.rem(zi, 2), zi // period
    per_pair = 4 * mem

    barrier = pltpu.get_barrier_semaphore()

    def greet_lon(k, _):
        pl.semaphore_signal(
            barrier, inc=1, device_id={"lon": lax.rem(zi + k, nz)}, device_id_type=MESH
        )
        return 0

    def greet_lat(k, _):
        pl.semaphore_signal(
            barrier, inc=1, device_id={"lat": lax.rem(mi + k, nm)}, device_id_type=MESH
        )
        return 0

    own = pl.ds(pl.multiple_of(mi * 128, 128), 128)
    zr_copy = pltpu.make_async_copy(zr_hbm, zr_ref, load_sem.at[2])
    mr_copy = pltpu.make_async_copy(mr_hbm.at[:, :, own], mr_ref, load_sem.at[3])
    x_copy = pltpu.make_async_copy(x_hbm, x_ref, load_sem.at[0])
    amp_copy = pltpu.make_async_copy(amp_hbm, amp_ref, load_sem.at[1])
    zr_copy.start()
    mr_copy.start()
    x_copy.start()
    amp_copy.start()
    lax.fori_loop(1, nz, greet_lon, 0)
    lax.fori_loop(1, nm, greet_lat, 0)

    zr_copy.wait()
    mr_copy.wait()
    a = jnp.concatenate([zr_ref[0], zr_ref[1], mr_ref[0], mr_ref[1]], axis=0)
    loss = 1.0 - a
    la = jnp.log(a)
    square = (128, 128)
    upto = jnp.where(row(square) <= lane(square), 1.0, 0.0)
    li = lax.dot_general(la, upto, NN, precision=HIGHEST, preferred_element_type=F32)
    lx = li - la
    total = li[:, 127:128]
    at = lane((8, 128))
    east_cols, west_cols, east_rows, west_rows = [], [], [], []
    for p in range(7):
        k = 2**p
        back = pltpu.roll(li, k, 1)
        ahead = pltpu.roll(li, 128 - k, 1)
        xback = pltpu.roll(lx, k, 1)
        xahead = pltpu.roll(lx, 128 - k, 1)
        first, last = at >= k, at < 128 - k
        east_cols.append((k, jnp.where(first, jnp.exp(jnp.where(first, li - back, 0.0)), 0.0)))
        east_rows.append((k, jnp.where(last, jnp.exp(jnp.where(last, ahead - li, 0.0)), 0.0)))
        west_cols.append((k, jnp.where(last, jnp.exp(jnp.where(last, xahead - lx, 0.0)), 0.0)))
        west_rows.append((k, jnp.where(first, jnp.exp(jnp.where(first, lx - xback, 0.0)), 0.0)))

    def rows_east(v):
        return loss * scan_lanes(v, east_rows, -1)

    def rows_west(v):
        return loss * scan_lanes(v, west_rows, 1)

    def cols_east(x):
        return scan_lanes(loss * x, east_cols, 1)

    def cols_west(x):
        return scan_lanes(loss * x, west_cols, -1)

    ge = jnp.exp(li)
    gw = jnp.exp(total - lx)
    v1 = jnp.exp(total - li) * loss
    w0 = jnp.exp(lx) * loss
    v2 = rows_east(w0)
    x1 = rows_west(v1)
    v3 = rows_east(x1)
    x2 = rows_west(v2)
    v4 = rows_east(x2)

    def along(v):
        return jnp.sum(v, axis=1, keepdims=True)

    kinds = (
        jnp.exp(total), along(w0 * ge), along(x1 * ge),
        along(v1 * gw), along(x2 * ge), along(v2 * gw),
    )
    packed = jnp.zeros((8, 128), F32)
    for k, value in enumerate(kinds):
        packed = jnp.where(at == k, value, packed)
    line = jnp.zeros((1, 128), F32)
    for n in range(4):
        mask = lane((1, 128)) // 8 == n
        line = jnp.where(mask, pltpu.roll(packed[n : n + 1], 8 * n, 1), line)
    kz_own[...] = line
    km_own[0:4] = packed[4:8]
    km_own[4:8] = packed[4:8]
    for f, v in enumerate((v1, v2, v3, v4)):
        for n in range(4):
            vz_ref[n * 4 + f : n * 4 + f + 1, :] = v[n : n + 1]
            vm_ref[n * 4 + f : n * 4 + f + 1, :] = v[4 + n : 5 + n]

    x_copy.wait()
    for l in range(2):
        both = [
            jnp.concatenate([ref[l * 4 : l * 4 + 4], ref[8 + l * 4 : 12 + l * 4]], axis=0)
            for ref in (vz_ref, vm_ref)
        ]
        zh, zl = halves(both[0])
        mh, ml = halves(both[1])
        z_wide = jnp.concatenate([zh, zl], axis=1)
        m_wide = jnp.concatenate([mh, ml], axis=1)

        def states(m, _):
            xh, xl = halves(x_ref[l, m])
            q = mul(z_wide, jnp.concatenate([xh, xh], axis=1), NT) + mul(zh, xl, NT)
            p = mul(m_wide, jnp.concatenate([xh, xh], axis=0), NN) + mul(mh, xl, NN)
            for s in range(2):
                base = (s * 2 + l) * per_pair
                qs[pl.ds(base + m * 4, 4), :] = q[s * 4 : s * 4 + 4]
                ps[pl.ds(base + m * 4, 4), :] = p[s * 4 : s * 4 + 4]
            return 0

        lax.fori_loop(0, mem, states, 0, unroll=16)

    u3 = cols_west(ge)
    u2 = cols_west(cols_east(gw))
    u1 = cols_west(cols_east(u3))
    for f, u in enumerate((u1, u2, u3, gw)):
        for n in range(4):
            uz_ref[n * 4 + f : n * 4 + f + 1, :] = u[n : n + 1]
            um_ref[n * 4 + f : n * 4 + f + 1, :] = u[4 + n : 5 + n]

    lit, lxt = jnp.transpose(li), jnp.transpose(lx)
    below = row(square) >= lane(square)
    above = row(square) <= lane(square)
    def matrices():
        for n in range(8):
            down = jnp.where(below, lit[:, n : n + 1] - li[n : n + 1], 0.0)
            up = jnp.where(above, lx[n : n + 1] - lxt[:, n : n + 1], 0.0)
            east = jnp.where(below, jnp.exp(down), 0.0) * loss[n : n + 1]
            west = jnp.where(above, jnp.exp(up), 0.0) * loss[n : n + 1]
            once = dot3(west, east, NN)
            high, low = halves(dot3(once, once, NN))
            if n < 4:
                s, l = n // 2, n % 2
                az_wide[l, s * 128 : s * 128 + 128, 0:128] = high
                az_wide[l, s * 128 : s * 128 + 128, 128:256] = high
                az_low[l, s * 128 : s * 128 + 128, :] = low
            else:
                am_wide[n - 4, :, 0:128] = high
                am_wide[n - 4, :, 128:256] = high
                am_low[n - 4] = low

    def local_pass(i, _):
        l, m = i // mem, lax.rem(i, mem)
        xh, xl = halves(x_ref[l, m])
        f = mul(jnp.concatenate([xh, xl], axis=1), az_wide[l], NT) + mul(xh, az_low[l], NT)
        for s in range(2):
            n = s * 2 + l
            fh, fl = halves(f[:, s * 128 : s * 128 + 128])
            field[n, m] = mul(am_wide[n], jnp.concatenate([fh, fl], axis=0), NN) + mul(
                am_low[n], fh, NN
            )
        return 0


    lead = jnp.where(early_side, jnp.where(z < (near + 3) // 4, lead0, lead1), 0)

    @pl.when(early_side)
    def _():
        matrices()

    def eight_passes(i, carry):
        for j in range(8):
            local_pass(8 * i + j, carry)
        return carry

    lax.fori_loop(0, lead, eight_passes, 0)

    pl.semaphore_wait(barrier, nz + nm - 2)

    def chunk(ref, index, size):
        return ref.at[pl.ds(pl.multiple_of(index * size, size), size), :]

    def remote(src, dst, which, **device):
        return pltpu.make_async_remote_copy(
            src_ref=src, dst_ref=dst,
            send_sem=send_sem.at[which], recv_sem=recv_sem.at[which],
            device_id=device, device_id_type=MESH,
        )

    other_z, other_m = lax.rem(zi + 1, nz), lax.rem(mi + 1, nm)

    def sent(ref, which):
        remote(ref, ref, which, lon=other_z).wait_send()

    def landed(ref, which):
        remote(ref, ref, which, lon=other_z).wait_recv()

    def first(ref, count):
        return ref.at[pl.ds(0, count)]

    def far_first(k):
        i = k // (2 * strips)
        half = (i + 1) // 2
        ahead = chips // 2 + jnp.where(lax.rem(i, 2) == 1, half, -half)
        there = lax.rem(z + ahead, chips)
        beside = lax.rem(core + lax.rem(k, 2), 2)
        return lax.rem(strip + lax.rem(k // 2, strips), strips) * period + there * 2 + beside

    def send_lon(k, _):
        d = far_first(k)

        @pl.when(d != zi)
        def _():
            remote(kz_own, kz_all.at[zi], 1, lon=d).start()
            remote(chunk(qs, d, zrows), chunk(qr, zi, zrows), 0, lon=d).start()

        return 0

    def send_lat(k, _):
        d = lax.rem(mi + k, nm)
        remote(chunk(ps, d, mrows), chunk(pr, mi, mrows), 2, lat=d).start()
        remote(km_own, chunk(km_all, mi, 8), 3, lat=d).start()
        return 0

    lax.fori_loop(0, nz, send_lon, 0)
    lax.fori_loop(1, nm, send_lat, 0)

    mine = jnp.concatenate(
        [ps[pl.ds(h * 128 + f, 32, stride=4), :] for h in range(2) for f in range(4)], axis=0
    )
    cross = dot3(vz_ref[...], mine, NT)
    wide = (16, rows)
    pair_of = lane(wide) // 128 * 2 + lane(wide) // mem % 2
    cross = jnp.where(row(wide) // 4 == pair_of, cross, 0.0)
    cross = cross[0:4] + cross[4:8] + cross[8:12] + cross[12:16]
    cs_own[0:4] = cross[:, 0:128]
    cs_own[4:8] = cross[:, 128:256]

    def send_states(k, _):
        d = far_first(k)

        @pl.when(d != zi)
        def _():
            remote(cs_own, chunk(cs_all, zi, 8), 7, lon=d).start()

        return 0

    lax.fori_loop(0, nz, send_states, 0)

    chunk(cs_all, zi, 8)[...] = cs_own[...]

    kz_all[zi] = kz_own[...]
    chunk(qr, zi, zrows)[...] = chunk(qs, zi, zrows)[...]

    chunk(pr, mi, mrows)[...] = chunk(ps, mi, mrows)[...]
    chunk(km_all, mi, 8)[...] = km_own[...]

    @pl.when(jnp.logical_not(early_side))
    def _():
        matrices()

    lax.fori_loop(lead, jnp.maximum(lead, split1), eight_passes, 0)

    zshape, mshape = (nz, 128), (nm, 128)
    early = lane((1, 128)) // mem % 2 == 0

    landed(first(pr, (nm - 1) * mrows), 2)
    landed(first(km_all, (nm - 1) * 8), 3)
    pair = mi * mrows // per_pair
    km = [km_all[pl.ds(n, nm, stride=8), :] for n in range(4)]
    own_km = km[0]
    for n in range(1, 4):
        own_km = jnp.where(pair == n, km[n], own_km)
    coupling = [jnp.broadcast_to(own_km[:, k : k + 1], mshape) for k in range(6)]
    groups = mrows // 4
    got = [
        [pr[pl.ds(g * 4 + f, nm, stride=mrows), :] for g in range(groups)] for f in range(4)
    ]
    for f, parts in enumerate(solve(got, coupling, nm, False)):
        for g in range(groups):
            prs[pl.ds(g * 4 + f, nm, stride=mrows), :] = parts[g]

    def back_lat(k, _):
        d = lax.rem(mi + k, nm)
        remote(chunk(prs, d, mrows), chunk(pin, mi, mrows), 5, lat=d).start()
        return 0

    lax.fori_loop(1, nm, back_lat, 0)
    chunk(pin, mi, mrows)[...] = chunk(prs, mi, mrows)[...]

    lax.fori_loop(jnp.maximum(lead, split1), jnp.maximum(lead, split2), eight_passes, 0)

    landed(kz_all.at[pl.ds(0, nz - 1)], 1)
    kz = kz_all[...].reshape(nz, 128)
    pair = zi * zrows // per_pair
    every = [
        [jnp.broadcast_to(kz[:, 8 * n + k : 8 * n + k + 1], zshape) for k in range(6)]
        for n in range(4)
    ]
    coupling = []
    for k in range(6):
        value = every[0][k]
        for n in range(1, 4):
            value = jnp.where(pair == n, every[n][k], value)
        coupling.append(value)
    landed(first(qr, (nz - 1) * zrows), 0)
    groups = zrows // 4
    got = [
        [qr[pl.ds(g * 4 + f, nz, stride=zrows), :] for g in range(groups)]
        for f in range(4)
    ]
    for f, parts in enumerate(solve(got, coupling, nz, True)):
        for g in range(groups):
            rs[pl.ds(g * 4 + f, nz, stride=zrows), :] = parts[g]

    def back_lon(k, _):
        there, turn = k // (2 * strips), lax.rem(k, 2 * strips)
        d = turn // 2 * period + there * 2 + lax.rem(turn, 2)

        @pl.when(d != zi)
        def _():
            remote(chunk(rs, d, zrows), chunk(rin, zi, zrows), 4, lon=d).start()

        return 0

    lax.fori_loop(0, nz, back_lon, 0)
    chunk(rin, zi, zrows)[...] = chunk(rs, zi, zrows)[...]


    landed(first(cs_all, (nz - 1) * 8), 7)
    for h in range(2):
        coupling = [
            jnp.where(early, every[2 * h][k], every[2 * h + 1][k]) for k in range(6)
        ]
        got = [[cs_all[pl.ds(h * 4 + f, nz, stride=8), :]] for f in range(4)]
        for f, parts in enumerate(solve(got, coupling, nz, True)):
            cz[h * 4 + f] = parts[0]

    for ref, block in ((crs, zi),):
        for h in range(2):
            tile = jnp.concatenate(
                [cz[h * 4 + f, pl.ds(block, 1), :] for f in range(4)] * 2, axis=0
            )
            turned = jnp.zeros((8, 128), F32)
            for d in range(4):
                moved = pltpu.roll(tile, (128 - 2 * mem * d) % 128, 1) if d else tile
                moved = pltpu.roll(moved, d, 0) if d else moved
                here = (row((8, 128)) - lane((8, 128)) // (2 * mem) + 8) % 4 == d
                turned = jnp.where(here, moved, turned)
            ref[h * 4 : h * 4 + 4, :] = turned[0:4]


    def send_cross(k, _):
        d = lax.rem(mi + k, nm)
        remote(crs, chunk(crr, mi, 8), 6, lat=d).start()
        return 0

    lax.fori_loop(1, nm, send_cross, 0)
    chunk(crr, mi, 8)[...] = crs[...]

    lax.fori_loop(jnp.maximum(lead, split2), mem // 4, eight_passes, 0)

    landed(first(pin, (nm - 1) * mrows), 5)
    for n in range(4):
        s, l = n // 2, n % 2
        part = slice(n * per_pair, (n + 1) * per_pair)
        ph, plow = halves(pin[part])
        d_ref[part] = mul(
            jnp.concatenate([ph, plow], axis=1), az_wide[l, s * 128 : s * 128 + 128, :], NT
        ) + mul(ph, az_low[l, s * 128 : s * 128 + 128, :], NT)
    amp_copy.wait()

    landed(first(rin, (nz - 1) * zrows), 4)

    for n in range(4):
        part = slice(n * per_pair, (n + 1) * per_pair)
        qh, ql = halves(rin[part])
        lq_ref[part] = mul(jnp.concatenate([qh, ql], axis=1), am_wide[n], NT) + mul(
            qh, am_low[n], NT
        )

    landed(first(crr, (nm - 1) * 8), 6)
    for h in range(2):
        coupling = [
            jnp.where(early, km[2 * h][:, k : k + 1], km[2 * h + 1][:, k : k + 1])
            for k in range(6)
        ]
        got = [[crr[pl.ds(h * 4 + f, nm, stride=8), :]] for f in range(4)]
        for f, parts in enumerate(solve(got, coupling, nm, False)):
            centre[h * 4 + f] = parts[0]
    for n in range(4):
        h = n // 2
        for f in range(4):
            line = centre[h * 4 + f, pl.ds(mi, 1), :]
            line = jnp.where(early if n % 2 == 0 else jnp.logical_not(early), line, 0.0)
            r = n * 4 + f
            cr_tile[r : r + 1, h * 128 : h * 128 + 128] = line
            cr_tile[r : r + 1, (1 - h) * 128 : (1 - h) * 128 + 128] = jnp.zeros((1, 128), F32)
    lr_ref[...] = dot3(cr_tile[...], um_ref[...], TN)

    sent(first(ps, (nm - 1) * mrows), 2)
    sent(first(km_all, (nm - 1) * 8), 3)
    sent(first(prs, (nm - 1) * mrows), 5)
    sent(first(crr, (nm - 1) * 8), 6)

    sent(first(qs, (nz - 1) * zrows), 0)
    sent(kz_all.at[pl.ds(0, nz - 1)], 1)
    sent(first(rs, (nz - 1) * zrows), 4)

    sent(first(cs_all, (nz - 1) * 8), 7)


def closing(
    mem, step, field, amp_ref, uz_ref, um_ref, lq_ref, lr_ref, d_ref, out_hbm, staged, store_sem
):
    per_pair = 4 * mem

    def finish(i):
        l, m = i // mem, lax.rem(i, mem)
        result = None
        for s in range(2):
            n = s * 2 + l
            part = pl.ds(n * per_pair + m * 4, 4)
            resp = pl.ds(n * 4, 4)
            entered = lr_ref[pl.ds(s * 128 + l * mem + m, 4, stride=2 * mem), :]
            left = jnp.concatenate([lq_ref[part, :] + entered, um_ref[resp, :]], axis=0)
            right = jnp.concatenate([uz_ref[resp, :], d_ref[part, :]], axis=0)
            lh = left.astype(BF16).astype(F32)
            rh = right.astype(BF16).astype(F32)
            stacked_left = jnp.concatenate([lh, left - lh, lh], axis=0).astype(BF16)
            stacked_right = jnp.concatenate([rh, rh, right - rh], axis=0).astype(BF16)
            y = field[n, m] + mul(stacked_left, stacked_right, TN)
            y = y * amp_ref[s, l]
            result = y if result is None else result + y
        staged[l, m] = result

    def put(i):
        part = pl.ds(lax.rem(i * step, mem), step)
        return pltpu.make_async_copy(
            staged.at[i * step // mem, part], out_hbm.at[i * step // mem, part], store_sem.at[i]
        )

    def several(i, _):
        for j in range(step):
            finish(step * i + j)
        put(i).start()
        return 0

    lax.fori_loop(0, 2 * mem // step, several, 0)
    for i in range(2 * mem // step):
        put(i).wait()


def body(nz, nm, perturbations, zonal_rate, meridional_rate, amplitude):
    mem = perturbations.shape[1]
    rows = 16 * mem
    vmem = pltpu.VMEM
    lead0, lead1, split1, split2 = 3, 1, 2, 3
    pieces = pl.pallas_call(
        functools.partial(kernel, nz, nm, mem, lead0, lead1, split1, split2),
        out_shape=[
            jax.ShapeDtypeStruct(shape, F32)
            for shape in (
                (4, mem, 128, 128), (2, 2, 128, 128), (16, 128), (16, 128),
                (rows, 128), (rows, 128), (rows, 128),
            )
        ],
        in_specs=[
            pl.BlockSpec(memory_space=pltpu.HBM) for _ in range(4)
        ],
        out_specs=[pl.BlockSpec(memory_space=pltpu.VMEM)] * 7,
        scratch_shapes=[
            vmem((2, mem, 128, 128), F32),
            vmem((2, 2, 128), F32), vmem((2, 2, 128), F32),
            vmem((16, 128), F32), vmem((16, 128), F32),
            vmem((2, 256, 256), BF16), vmem((2, 256, 128), BF16),
            vmem((4, 128, 256), BF16), vmem((4, 128, 128), BF16),
            *[vmem((rows, 128), F32) for _ in range(8)],
            vmem((1, 128), F32), vmem((nz, 1, 128), F32),
            vmem((8, 128), F32), vmem((8 * nm, 128), F32),
            vmem((8, 128), F32), vmem((8 * nz, 128), F32), vmem((8, nz, 128), F32),
            vmem((8, 128), F32), vmem((8 * nm, 128), F32),
            vmem((8, nm, 128), F32),
            vmem((16, 256), F32),
            pltpu.SemaphoreType.DMA((4,)),
            pltpu.SemaphoreType.DMA((9,)),
            pltpu.SemaphoreType.DMA((9,)),
        ],
        compiler_params=pltpu.CompilerParams(
            collective_id=0, has_side_effects=True, vmem_limit_bytes=48 * 1024 * 1024
        ),
    )(*(pltpu.with_memory_space_constraint(v, pltpu.HBM) for v in (perturbations, zonal_rate, meridional_rate, amplitude)))
    step = 8
    return pl.pallas_call(
        functools.partial(closing, mem, step),
        out_shape=jax.ShapeDtypeStruct(perturbations.shape, F32),
        in_specs=[pl.BlockSpec(memory_space=pltpu.VMEM)] * 7,
        out_specs=pl.BlockSpec(memory_space=pltpu.HBM),
        scratch_shapes=[
            vmem(perturbations.shape, F32), pltpu.SemaphoreType.DMA((2 * mem // step,)),
        ],
        compiler_params=pltpu.CompilerParams(vmem_limit_bytes=32 * 1024 * 1024),
    )(*pieces)


def solution(mesh):
    spec = P(None, None, "lat", "lon")
    return jax.shard_map(
        functools.partial(body, mesh.shape["lon"], mesh.shape["lat"]),
        mesh=mesh,
        in_specs=(spec, P(None, None, "lon"), P(), spec),
        out_specs=spec,
        check_vma=False,
    )
```

```python
import functools

import jax
import jax.numpy as jnp
from jax import lax
from jax.experimental import pallas as pl
from jax.experimental.pallas import tpu as pltpu
from jax.sharding import PartitionSpec as P

MESH = pl.DeviceIdType.MESH
F32, BF16 = jnp.float32, jnp.bfloat16
HIGHEST = lax.Precision.HIGHEST

NN = (((1,), (0,)), ((), ()))
NT = (((1,), (1,)), ((), ()))
TN = (((0,), (0,)), ((), ()))


def halves(x):
    high = x.astype(BF16)
    return high, (x - high.astype(F32)).astype(BF16)


def mul(a, b, dims):
    return lax.dot_general(a, b, dims, preferred_element_type=F32)


def dot3(a, b, dims):
    ah, al = halves(a)
    bh, bl = halves(b)
    ka, kb = dims[0][0][0], dims[0][1][0]
    return mul(jnp.concatenate([ah, al], ka), jnp.concatenate([bh, bh], kb), dims) + mul(
        ah, bl, dims
    )


def lane(shape):
    return lax.broadcasted_iota(jnp.int32, shape, 1)


def row(shape):
    return lax.broadcasted_iota(jnp.int32, shape, 0)


def scan_lanes(v, steps, sign):
    width = v.shape[1]
    for k, factor in steps:
        v = v + factor * pltpu.roll(v, k if sign > 0 else width - k, 1)
    return v


def solve(states, coupling, blocks, cyclic):
    g, r, e1e2, w1e2, e1w2, w1w2 = coupling
    shape = (blocks, 128)
    at = row(shape)
    levels = blocks.bit_length() - 1

    def shifted(x, k):
        moved = pltpu.roll(x, k % blocks, 0)
        if cyclic:
            return moved
        return jnp.where((at >= k) if k > 0 else (at < blocks + k), moved, 0.0)

    factors = {}
    for sign in (1, -1):
        a = pltpu.roll(g, sign % blocks, 0)
        factors[sign] = []
        for level in range(levels):
            factors[sign].append(a)
            a = a * pltpu.roll(a, (sign * 2**level) % blocks, 0)
        factors[sign].append(1.0 / (1.0 - a) if cyclic else None)

    def carry(parts, sign):
        out = []
        for v in parts:
            v = shifted(v, sign)
            for level in range(levels):
                v = v + factors[sign][level] * shifted(v, sign * 2**level)
            out.append(v * factors[sign][levels] if cyclic else v)
        return out

    n = len(states[0])
    e1 = carry(states[0], 1)
    w1 = carry([states[1][i] + r * e1[i] for i in range(n)], -1)
    e2 = carry([states[2][i] + e1e2 * e1[i] + w1e2 * w1[i] for i in range(n)], 1)
    w2 = carry(
        [states[3][i] + e1w2 * e1[i] + w1w2 * w1[i] + r * e2[i] for i in range(n)], -1
    )
    return e1, w1, e2, w2


def kernel(
    nz, nm, mem, lead0, lead1, split1, split2,
    x_hbm, zr_hbm, mr_hbm, amp_hbm,
    field, amp_ref, uz_ref, um_ref, lq_ref, lr_ref, d_ref,
    x_ref, zr_ref, mr_ref, vz_ref, vm_ref,
    az_wide, az_low, am_wide, am_low,
    qs, rin, ps, pr, prs, pin, qr, rs,
    kz_own, kz_all, km_own, km_all, cs_own, cs_all, cz, crs, crr, centre,
    cr_tile,
    load_sem, send_sem, recv_sem,
):
    zi, mi = lax.axis_index("lon"), lax.axis_index("lat")
    rows = 16 * mem
    period = min(nz, 16)
    near, chips, strips = period // 2, period // 2, nz // period
    early_side = lax.rem(zi, period) < near
    zrows, mrows = rows // nz, rows // nm
    z, core, strip = lax.rem(zi, period) // 2, lax.rem(zi, 2), zi // period
    per_pair = 4 * mem

    barrier = pltpu.get_barrier_semaphore()

    def greet_lon(k, _):
        pl.semaphore_signal(
            barrier, inc=1, device_id={"lon": lax.rem(zi + k, nz)}, device_id_type=MESH
        )
        return 0

    def greet_lat(k, _):
        pl.semaphore_signal(
            barrier, inc=1, device_id={"lat": lax.rem(mi + k, nm)}, device_id_type=MESH
        )
        return 0

    own = pl.ds(pl.multiple_of(mi * 128, 128), 128)
    zr_copy = pltpu.make_async_copy(zr_hbm, zr_ref, load_sem.at[2])
    mr_copy = pltpu.make_async_copy(mr_hbm.at[:, :, own], mr_ref, load_sem.at[3])
    x_copy = pltpu.make_async_copy(x_hbm, x_ref, load_sem.at[0])
    amp_copy = pltpu.make_async_copy(amp_hbm, amp_ref, load_sem.at[1])
    zr_copy.start()
    mr_copy.start()
    x_copy.start()
    amp_copy.start()
    lax.fori_loop(1, nz, greet_lon, 0)
    lax.fori_loop(1, nm, greet_lat, 0)

    zr_copy.wait()
    mr_copy.wait()
    a = jnp.concatenate([zr_ref[0], zr_ref[1], mr_ref[0], mr_ref[1]], axis=0)
    loss = 1.0 - a
    la = jnp.log(a)
    square = (128, 128)
    upto = jnp.where(row(square) <= lane(square), 1.0, 0.0)
    li = lax.dot_general(la, upto, NN, precision=HIGHEST, preferred_element_type=F32)
    lx = li - la
    total = li[:, 127:128]
    at = lane((8, 128))
    east_cols, west_cols, east_rows, west_rows = [], [], [], []
    for p in range(7):
        k = 2**p
        back = pltpu.roll(li, k, 1)
        ahead = pltpu.roll(li, 128 - k, 1)
        xback = pltpu.roll(lx, k, 1)
        xahead = pltpu.roll(lx, 128 - k, 1)
        first, last = at >= k, at < 128 - k
        east_cols.append((k, jnp.where(first, jnp.exp(jnp.where(first, li - back, 0.0)), 0.0)))
        east_rows.append((k, jnp.where(last, jnp.exp(jnp.where(last, ahead - li, 0.0)), 0.0)))
        west_cols.append((k, jnp.where(last, jnp.exp(jnp.where(last, xahead - lx, 0.0)), 0.0)))
        west_rows.append((k, jnp.where(first, jnp.exp(jnp.where(first, lx - xback, 0.0)), 0.0)))

    def rows_east(v):
        return loss * scan_lanes(v, east_rows, -1)

    def rows_west(v):
        return loss * scan_lanes(v, west_rows, 1)

    def cols_east(x):
        return scan_lanes(loss * x, east_cols, 1)

    def cols_west(x):
        return scan_lanes(loss * x, west_cols, -1)

    ge = jnp.exp(li)
    gw = jnp.exp(total - lx)
    v1 = jnp.exp(total - li) * loss
    w0 = jnp.exp(lx) * loss
    v2 = rows_east(w0)
    x1 = rows_west(v1)
    v3 = rows_east(x1)
    x2 = rows_west(v2)
    v4 = rows_east(x2)

    def along(v):
        return jnp.sum(v, axis=1, keepdims=True)

    kinds = (
        jnp.exp(total), along(w0 * ge), along(x1 * ge),
        along(v1 * gw), along(x2 * ge), along(v2 * gw),
    )
    packed = jnp.zeros((8, 128), F32)
    for k, value in enumerate(kinds):
        packed = jnp.where(at == k, value, packed)
    line = jnp.zeros((1, 128), F32)
    for n in range(4):
        mask = lane((1, 128)) // 8 == n
        line = jnp.where(mask, pltpu.roll(packed[n : n + 1], 8 * n, 1), line)
    kz_own[...] = line
    km_own[0:4] = packed[4:8]
    km_own[4:8] = packed[4:8]
    for f, v in enumerate((v1, v2, v3, v4)):
        for n in range(4):
            vz_ref[n * 4 + f : n * 4 + f + 1, :] = v[n : n + 1]
            vm_ref[n * 4 + f : n * 4 + f + 1, :] = v[4 + n : 5 + n]

    x_copy.wait()
    for l in range(2):
        both = [
            jnp.concatenate([ref[l * 4 : l * 4 + 4], ref[8 + l * 4 : 12 + l * 4]], axis=0)
            for ref in (vz_ref, vm_ref)
        ]
        zh, zl = halves(both[0])
        mh, ml = halves(both[1])
        z_wide = jnp.concatenate([zh, zl], axis=1)
        m_wide = jnp.concatenate([mh, ml], axis=1)

        def states(m, _):
            xh, xl = halves(x_ref[l, m])
            q = mul(z_wide, jnp.concatenate([xh, xh], axis=1), NT) + mul(zh, xl, NT)
            p = mul(m_wide, jnp.concatenate([xh, xh], axis=0), NN) + mul(mh, xl, NN)
            for s in range(2):
                base = (s * 2 + l) * per_pair
                qs[pl.ds(base + m * 4, 4), :] = q[s * 4 : s * 4 + 4]
                ps[pl.ds(base + m * 4, 4), :] = p[s * 4 : s * 4 + 4]
            return 0

        lax.fori_loop(0, mem, states, 0, unroll=16)

    u3 = cols_west(ge)
    u2 = cols_west(cols_east(gw))
    u1 = cols_west(cols_east(u3))
    for f, u in enumerate((u1, u2, u3, gw)):
        for n in range(4):
            uz_ref[n * 4 + f : n * 4 + f + 1, :] = u[n : n + 1]
            um_ref[n * 4 + f : n * 4 + f + 1, :] = u[4 + n : 5 + n]

    lit, lxt = jnp.transpose(li), jnp.transpose(lx)
    below = row(square) >= lane(square)
    above = row(square) <= lane(square)
    def matrices():
        for n in range(8):
            down = jnp.where(below, lit[:, n : n + 1] - li[n : n + 1], 0.0)
            up = jnp.where(above, lx[n : n + 1] - lxt[:, n : n + 1], 0.0)
            east = jnp.where(below, jnp.exp(down), 0.0) * loss[n : n + 1]
            west = jnp.where(above, jnp.exp(up), 0.0) * loss[n : n + 1]
            once = dot3(west, east, NN)
            high, low = halves(dot3(once, once, NN))
            if n < 4:
                s, l = n // 2, n % 2
                az_wide[l, s * 128 : s * 128 + 128, 0:128] = high
                az_wide[l, s * 128 : s * 128 + 128, 128:256] = high
                az_low[l, s * 128 : s * 128 + 128, :] = low
            else:
                am_wide[n - 4, :, 0:128] = high
                am_wide[n - 4, :, 128:256] = high
                am_low[n - 4] = low

    def local_pass(i, _):
        l, m = i // mem, lax.rem(i, mem)
        xh, xl = halves(x_ref[l, m])
        f = mul(jnp.concatenate([xh, xl], axis=1), az_wide[l], NT) + mul(xh, az_low[l], NT)
        for s in range(2):
            n = s * 2 + l
            fh, fl = halves(f[:, s * 128 : s * 128 + 128])
            field[n, m] = mul(am_wide[n], jnp.concatenate([fh, fl], axis=0), NN) + mul(
                am_low[n], fh, NN
            )
        return 0


    mine = jnp.concatenate(
        [ps[pl.ds(h * 128 + f, 32, stride=4), :] for h in range(2) for f in range(4)], axis=0
    )
    cross = dot3(vz_ref[...], mine, NT)
    wide = (16, rows)
    pair_of = lane(wide) // 128 * 2 + lane(wide) // mem % 2
    cross = jnp.where(row(wide) // 4 == pair_of, cross, 0.0)
    cross = cross[0:4] + cross[4:8] + cross[8:12] + cross[12:16]
    cs_own[0:4] = cross[:, 0:128]
    cs_own[4:8] = cross[:, 128:256]

    lead = jnp.where(early_side, jnp.where(z < (near + 3) // 4, lead0, lead1), 0)

    @pl.when(early_side)
    def _():
        matrices()

    def eight_passes(i, carry):
        for j in range(8):
            local_pass(8 * i + j, carry)
        return carry

    lax.fori_loop(0, lead, eight_passes, 0)

    pl.semaphore_wait(barrier, nz + nm - 2)

    def chunk(ref, index, size):
        return ref.at[pl.ds(pl.multiple_of(index * size, size), size), :]

    def remote(src, dst, which, **device):
        return pltpu.make_async_remote_copy(
            src_ref=src, dst_ref=dst,
            send_sem=send_sem.at[which], recv_sem=recv_sem.at[which],
            device_id=device, device_id_type=MESH,
        )

    other_z, other_m = lax.rem(zi + 1, nz), lax.rem(mi + 1, nm)

    def sent(ref, which):
        remote(ref, ref, which, lon=other_z).wait_send()

    def landed(ref, which):
        remote(ref, ref, which, lon=other_z).wait_recv()

    def first(ref, count):
        return ref.at[pl.ds(0, count)]

    def far_first(k):
        i = k // (2 * strips)
        half = (i + 1) // 2
        ahead = chips // 2 + jnp.where(lax.rem(i, 2) == 1, half, -half)
        there = lax.rem(z + ahead, chips)
        beside = lax.rem(core + lax.rem(k, 2), 2)
        return lax.rem(strip + lax.rem(k // 2, strips), strips) * period + there * 2 + beside

    def send_lon(k, _):
        d = far_first(k)

        @pl.when(d != zi)
        def _():
            remote(kz_own, kz_all.at[zi], 1, lon=d).start()
            remote(chunk(qs, d, zrows), chunk(qr, zi, zrows), 0, lon=d).start()

        return 0

    def send_lat(k, _):
        d = lax.rem(mi + k, nm)
        remote(chunk(ps, d, mrows), chunk(pr, mi, mrows), 2, lat=d).start()
        remote(km_own, chunk(km_all, mi, 8), 3, lat=d).start()
        return 0

    lax.fori_loop(1, nm, send_lat, 0)
    lax.fori_loop(0, nz, send_lon, 0)

    def send_states(k, _):
        d = far_first(k)

        @pl.when(d != zi)
        def _():
            remote(cs_own, chunk(cs_all, zi, 8), 7, lon=d).start()

        return 0

    lax.fori_loop(0, nz, send_states, 0)

    chunk(cs_all, zi, 8)[...] = cs_own[...]

    kz_all[zi] = kz_own[...]
    chunk(qr, zi, zrows)[...] = chunk(qs, zi, zrows)[...]

    chunk(pr, mi, mrows)[...] = chunk(ps, mi, mrows)[...]
    chunk(km_all, mi, 8)[...] = km_own[...]

    @pl.when(jnp.logical_not(early_side))
    def _():
        matrices()

    lax.fori_loop(lead, jnp.maximum(lead, split1), eight_passes, 0)

    zshape, mshape = (nz, 128), (nm, 128)
    early = lane((1, 128)) // mem % 2 == 0

    landed(first(pr, (nm - 1) * mrows), 2)
    landed(first(km_all, (nm - 1) * 8), 3)
    pair = mi * mrows // per_pair
    km = [km_all[pl.ds(n, nm, stride=8), :] for n in range(4)]
    own_km = km[0]
    for n in range(1, 4):
        own_km = jnp.where(pair == n, km[n], own_km)
    coupling = [jnp.broadcast_to(own_km[:, k : k + 1], mshape) for k in range(6)]
    groups = mrows // 4
    got = [
        [pr[pl.ds(g * 4 + f, nm, stride=mrows), :] for g in range(groups)] for f in range(4)
    ]
    for f, parts in enumerate(solve(got, coupling, nm, False)):
        for g in range(groups):
            prs[pl.ds(g * 4 + f, nm, stride=mrows), :] = parts[g]

    def back_lat(k, _):
        d = lax.rem(mi + k, nm)
        remote(chunk(prs, d, mrows), chunk(pin, mi, mrows), 5, lat=d).start()
        return 0

    lax.fori_loop(1, nm, back_lat, 0)
    chunk(pin, mi, mrows)[...] = chunk(prs, mi, mrows)[...]

    lax.fori_loop(jnp.maximum(lead, split1), jnp.maximum(lead, split2), eight_passes, 0)

    landed(kz_all.at[pl.ds(0, nz - 1)], 1)
    kz = kz_all[...].reshape(nz, 128)
    pair = zi * zrows // per_pair
    every = [
        [jnp.broadcast_to(kz[:, 8 * n + k : 8 * n + k + 1], zshape) for k in range(6)]
        for n in range(4)
    ]
    coupling = []
    for k in range(6):
        value = every[0][k]
        for n in range(1, 4):
            value = jnp.where(pair == n, every[n][k], value)
        coupling.append(value)
    landed(first(qr, (nz - 1) * zrows), 0)
    groups = zrows // 4
    got = [
        [qr[pl.ds(g * 4 + f, nz, stride=zrows), :] for g in range(groups)]
        for f in range(4)
    ]
    for f, parts in enumerate(solve(got, coupling, nz, True)):
        for g in range(groups):
            rs[pl.ds(g * 4 + f, nz, stride=zrows), :] = parts[g]

    def back_lon(k, _):
        there, turn = k // (2 * strips), lax.rem(k, 2 * strips)
        d = turn // 2 * period + there * 2 + lax.rem(turn, 2)

        @pl.when(d != zi)
        def _():
            remote(chunk(rs, d, zrows), chunk(rin, zi, zrows), 4, lon=d).start()

        return 0

    lax.fori_loop(0, nz, back_lon, 0)
    chunk(rin, zi, zrows)[...] = chunk(rs, zi, zrows)[...]


    landed(first(cs_all, (nz - 1) * 8), 7)
    for h in range(2):
        coupling = [
            jnp.where(early, every[2 * h][k], every[2 * h + 1][k]) for k in range(6)
        ]
        got = [[cs_all[pl.ds(h * 4 + f, nz, stride=8), :]] for f in range(4)]
        for f, parts in enumerate(solve(got, coupling, nz, True)):
            cz[h * 4 + f] = parts[0]

    for ref, block in ((crs, zi),):
        for h in range(2):
            tile = jnp.concatenate(
                [cz[h * 4 + f, pl.ds(block, 1), :] for f in range(4)] * 2, axis=0
            )
            turned = jnp.zeros((8, 128), F32)
            for d in range(4):
                moved = pltpu.roll(tile, (128 - 2 * mem * d) % 128, 1) if d else tile
                moved = pltpu.roll(moved, d, 0) if d else moved
                here = (row((8, 128)) - lane((8, 128)) // (2 * mem) + 8) % 4 == d
                turned = jnp.where(here, moved, turned)
            ref[h * 4 : h * 4 + 4, :] = turned[0:4]


    def send_cross(k, _):
        d = lax.rem(mi + k, nm)
        remote(crs, chunk(crr, mi, 8), 6, lat=d).start()
        return 0

    lax.fori_loop(1, nm, send_cross, 0)
    chunk(crr, mi, 8)[...] = crs[...]

    lax.fori_loop(jnp.maximum(lead, split2), mem // 4, eight_passes, 0)

    landed(first(pin, (nm - 1) * mrows), 5)
    for n in range(4):
        s, l = n // 2, n % 2
        part = slice(n * per_pair, (n + 1) * per_pair)
        ph, plow = halves(pin[part])
        d_ref[part] = mul(
            jnp.concatenate([ph, plow], axis=1), az_wide[l, s * 128 : s * 128 + 128, :], NT
        ) + mul(ph, az_low[l, s * 128 : s * 128 + 128, :], NT)
    amp_copy.wait()

    landed(first(rin, (nz - 1) * zrows), 4)

    for n in range(4):
        part = slice(n * per_pair, (n + 1) * per_pair)
        qh, ql = halves(rin[part])
        lq_ref[part] = mul(jnp.concatenate([qh, ql], axis=1), am_wide[n], NT) + mul(
            qh, am_low[n], NT
        )

    landed(first(crr, (nm - 1) * 8), 6)
    for h in range(2):
        coupling = [
            jnp.where(early, km[2 * h][:, k : k + 1], km[2 * h + 1][:, k : k + 1])
            for k in range(6)
        ]
        got = [[crr[pl.ds(h * 4 + f, nm, stride=8), :]] for f in range(4)]
        for f, parts in enumerate(solve(got, coupling, nm, False)):
            centre[h * 4 + f] = parts[0]
    for n in range(4):
        h = n // 2
        for f in range(4):
            line = centre[h * 4 + f, pl.ds(mi, 1), :]
            line = jnp.where(early if n % 2 == 0 else jnp.logical_not(early), line, 0.0)
            r = n * 4 + f
            cr_tile[r : r + 1, h * 128 : h * 128 + 128] = line
            cr_tile[r : r + 1, (1 - h) * 128 : (1 - h) * 128 + 128] = jnp.zeros((1, 128), F32)
    lr_ref[...] = dot3(cr_tile[...], um_ref[...], TN)

    sent(first(ps, (nm - 1) * mrows), 2)
    sent(first(km_all, (nm - 1) * 8), 3)
    sent(first(prs, (nm - 1) * mrows), 5)
    sent(first(crr, (nm - 1) * 8), 6)

    sent(first(qs, (nz - 1) * zrows), 0)
    sent(kz_all.at[pl.ds(0, nz - 1)], 1)
    sent(first(rs, (nz - 1) * zrows), 4)

    sent(first(cs_all, (nz - 1) * 8), 7)


def closing(
    mem, step, field, amp_ref, uz_ref, um_ref, lq_ref, lr_ref, d_ref, out_hbm, staged, store_sem
):
    per_pair = 4 * mem

    def finish(i):
        l, m = i // mem, lax.rem(i, mem)
        result = None
        for s in range(2):
            n = s * 2 + l
            part = pl.ds(n * per_pair + m * 4, 4)
            resp = pl.ds(n * 4, 4)
            entered = lr_ref[pl.ds(s * 128 + l * mem + m, 4, stride=2 * mem), :]
            left = jnp.concatenate([lq_ref[part, :] + entered, um_ref[resp, :]], axis=0)
            right = jnp.concatenate([uz_ref[resp, :], d_ref[part, :]], axis=0)
            lh = left.astype(BF16).astype(F32)
            rh = right.astype(BF16).astype(F32)
            stacked_left = jnp.concatenate([lh, left - lh, lh], axis=0).astype(BF16)
            stacked_right = jnp.concatenate([rh, rh, right - rh], axis=0).astype(BF16)
            y = field[n, m] + mul(stacked_left, stacked_right, TN)
            y = y * amp_ref[s, l]
            result = y if result is None else result + y
        staged[l, m] = result

    def put(i):
        half = step // 2
        part = pl.ds(lax.rem(i * half, mem), half)
        return pltpu.make_async_copy(
            staged.at[i * half // mem, part], out_hbm.at[i * half // mem, part], store_sem.at[i]
        )

    def several(i, _):
        for part in range(2):
            for j in range(step // 2):
                finish(step * i + step // 2 * part + j)
            put(2 * i + part).start()
        return 0

    lax.fori_loop(0, 2 * mem // step, several, 0)
    for i in range(4 * mem // step):
        put(i).wait()


def body(nz, nm, perturbations, zonal_rate, meridional_rate, amplitude):
    mem = perturbations.shape[1]
    rows = 16 * mem
    vmem = pltpu.VMEM
    lead0, lead1, split1, split2 = 2, 1, 2, 2
    pieces = pl.pallas_call(
        functools.partial(kernel, nz, nm, mem, lead0, lead1, split1, split2),
        out_shape=[
            jax.ShapeDtypeStruct(shape, F32)
            for shape in (
                (4, mem, 128, 128), (2, 2, 128, 128), (16, 128), (16, 128),
                (rows, 128), (rows, 128), (rows, 128),
            )
        ],
        in_specs=[
            pl.BlockSpec(memory_space=pltpu.HBM) for _ in range(4)
        ],
        out_specs=[pl.BlockSpec(memory_space=pltpu.VMEM)] * 7,
        scratch_shapes=[
            vmem((2, mem, 128, 128), F32),
            vmem((2, 2, 128), F32), vmem((2, 2, 128), F32),
            vmem((16, 128), F32), vmem((16, 128), F32),
            vmem((2, 256, 256), BF16), vmem((2, 256, 128), BF16),
            vmem((4, 128, 256), BF16), vmem((4, 128, 128), BF16),
            *[vmem((rows, 128), F32) for _ in range(8)],
            vmem((1, 128), F32), vmem((nz, 1, 128), F32),
            vmem((8, 128), F32), vmem((8 * nm, 128), F32),
            vmem((8, 128), F32), vmem((8 * nz, 128), F32), vmem((8, nz, 128), F32),
            vmem((8, 128), F32), vmem((8 * nm, 128), F32),
            vmem((8, nm, 128), F32),
            vmem((16, 256), F32),
            pltpu.SemaphoreType.DMA((4,)),
            pltpu.SemaphoreType.DMA((9,)),
            pltpu.SemaphoreType.DMA((9,)),
        ],
        compiler_params=pltpu.CompilerParams(
            collective_id=0, has_side_effects=True, vmem_limit_bytes=48 * 1024 * 1024
        ),
    )(*(pltpu.with_memory_space_constraint(v, pltpu.HBM) for v in (perturbations, zonal_rate, meridional_rate, amplitude)))
    step = 8
    return pl.pallas_call(
        functools.partial(closing, mem, step),
        out_shape=jax.ShapeDtypeStruct(perturbations.shape, F32),
        in_specs=[pl.BlockSpec(memory_space=pltpu.VMEM)] * 7,
        out_specs=pl.BlockSpec(memory_space=pltpu.HBM),
        scratch_shapes=[
            vmem(perturbations.shape, F32), pltpu.SemaphoreType.DMA((4 * mem // step,)),
        ],
        compiler_params=pltpu.CompilerParams(vmem_limit_bytes=32 * 1024 * 1024),
    )(*pieces)


def solution(mesh):
    spec = P(None, None, "lat", "lon")
    return jax.shard_map(
        functools.partial(body, mesh.shape["lon"], mesh.shape["lat"]),
        mesh=mesh,
        in_specs=(spec, P(None, None, "lon"), P(), spec),
        out_specs=spec,
        check_vma=False,
    )
```
